32 devices in a mesh: lat: 4 (over y, x), lev: 8 (over z, core).
Axes of the slice: x: 2, y: 2, z: 4, core: 2. Of those that a mesh axis runs over, the one named last changes fastest.
Arguments:
- state: float32 [6, 12, 32, 1152], P(None, 'lat', 'lev'), may hold values from -6 to 6
- courant: float32 [2, 12, 32, 1152], P(None, 'lat', 'lev'), may hold values from -0.4 to 0.4
- offsets: int32 [2, 12, 32, 1152], P(None, 'lat', 'lev'), may hold values from -1 to 2
- log_thickness: float32 [12, 32, 1152], P('lat', 'lev'), may hold values from 0.05 to 0.5
- surface: float32 [12, 1152], P('lat'), may hold values from -6 to 6
- remap_level: int32 [12, 32, 1152], P('lat', None, 'lev'), may hold values from 0 to 31, as said below
- remap_weight: float32 [12, 32, 1152], P('lat', None, 'lev'), may hold values from 0 to 1
Outputs:
- remapped: float32 [6, 12, 32, 1152], P(None, 'lat', 'lev')
- geopotential: float32 [12, 32, 1152], P('lat', 'lev')
The draws below stay inside these ranges and needn't reach their ends.
Inputs may be any that keep to these rules, and one draw needn't show every extreme that they name: `remap_level`: the source level of target level k lies within 2 of k.
All inputs are finite; a program needn't handle non-finite values.
Results may differ from the reference program's by a relative error of at most 0.00007.
Values sent between devices are 32-bit elements; how exact they have to be, the bound alone decides.
A program may use at most 64 MiB of HBM per device.

```python
import math
import jax
import jax.numpy as jnp
from jax import lax

NLON = 1152
SUBSTEPS = 2
FIELDS = 6
NLAT = 12
LEV = 32


def draw_remap_level(key, part):
    spread = jax.random.randint(key, (NLAT, LEV, NLON), -2, 3, dtype=jnp.int32)
    levels = jnp.arange(LEV, dtype=jnp.int32)[None, :, None]
    return jnp.clip(levels + spread, 0, LEV - 1).astype(jnp.int32)


def place_ends(array, stream_key, least, top_value):
    extent = array.shape
    index_at = [jax.random.randint(jax.random.fold_in(stream_key, axis), (), 0, extent[axis]) for axis in range(len(extent))]
    array = array.at[tuple(index_at)].set(least)
    longest = extent.index(max(extent))
    index_at[longest] = (index_at[longest] + 1) % extent[longest]
    return array.at[tuple(index_at)].set(top_value)


def level_of(own_key, extent, shards, smallest, largest):
    def one(axis_at, shards_of):
        steps = jax.random.uniform(jax.random.fold_in(jax.random.fold_in(own_key, 6), axis_at), (shards_of,), jnp.float32, smallest / len(shards), largest / len(shards))
        return jnp.repeat(jnp.exp(steps), extent[axis_at] // shards_of).reshape((-1,) + (1,) * (len(extent) - axis_at - 1))

    factor_of = one(*shards[0])
    for cut in shards[1:]:
        factor_of = factor_of * one(*cut)
    return factor_of


def gaussian(stream_key, shape, scale, most, pieces=(), kind=jnp.bfloat16):
    result = jax.random.normal(stream_key, shape, jnp.float32) * scale
    if len(pieces) > 0:
        result = level_of(stream_key, shape, pieces, -0.22, 0.18) * result
    return jnp.clip(result, min=-most, max=most).astype(kind)


def setup_inputs(seed: int = 0) -> dict:
    key_list = jax.random.split(jax.random.key(seed), 8)
    state = gaussian(key_list[0], (FIELDS, NLAT, LEV, NLON), 1.0, 6.0, ((1, 4), (2, 8)), jnp.float32)
    courant = jnp.clip(jax.random.uniform(key_list[1], (2, NLAT, LEV, NLON), jnp.float32, -0.4, 0.4) * level_of(key_list[1], (2, NLAT, LEV, NLON), ((1, 4), (2, 8)), -0.4, 0.0), -0.4, 0.4)
    offsets = place_ends(jax.random.randint(key_list[2], (2, NLAT, LEV, NLON), -1, 3), jax.random.fold_in(key_list[2], 1), -1, 2).astype(jnp.int32)
    log_thickness = jnp.clip(jnp.exp(math.log(0.5) - 2.3025851 * jax.random.uniform(key_list[3], (NLAT, LEV, NLON), jnp.float32) ** level_of(key_list[3], (NLAT, LEV, NLON), ((0, 4), (1, 8)), -0.2, 0.2)), 0.05, 0.5)
    surface = gaussian(key_list[4], (NLAT, NLON), 1.0, 6.0, ((0, 4),), jnp.float32)
    remap_level = draw_remap_level(jax.random.fold_in(key_list[7], 71), 0)
    remap_weight = jnp.clip(1.0 * jax.random.uniform(key_list[6], (NLAT, LEV, NLON), jnp.float32) ** level_of(key_list[6], (NLAT, LEV, NLON), ((0, 4), (2, 8)), -0.2, 0.2), 0.0, 1.0)
    return {"state": state, "courant": courant, "offsets": offsets, "log_thickness": log_thickness, "surface": surface, "remap_level": remap_level, "remap_weight": remap_weight}


def parabola(q, source, weight):
    n = q.shape[-2]
    widths = [(0, 0)] * (q.ndim - 2) + [(2, 2), (0, 0)]
    padded = jnp.pad(q, widths, mode="edge")
    edges = (7.0 * (padded[..., 1:n + 2, :] + padded[..., 2:n + 3, :]) - (padded[..., 0:n + 1, :] + padded[..., 3:n + 4, :])) / 12.0
    centre = jnp.take_along_axis(q, source, axis=-2)
    left = jnp.take_along_axis(edges[..., :n, :], source, axis=-2)
    right = jnp.take_along_axis(edges[..., 1:, :], source, axis=-2)
    slope = right - left
    curve = 6.0 * centre - 3.0 * (left + right)
    return left + weight * (slope + curve * (1.0 - weight))


def reference(state, courant, offsets, log_thickness, surface, remap_level, remap_weight):
    rows = state.shape[1]
    width = state.shape[3]
    row_index = jnp.arange(rows, dtype=jnp.int32)[:, None, None]
    north_index = row_index + offsets[0] + 2
    east_index = (jnp.arange(width, dtype=jnp.int32)[None, None, :] + offsets[1]) % width

    def advect(q):
        for substep in range(SUBSTEPS):
            padded = jnp.pad(q, ((2, 2), (0, 0), (0, 0)))
            north = courant[0] * jnp.take_along_axis(padded, north_index, axis=0)
            south = jnp.concatenate([jnp.zeros_like(north[:1]), north[:-1]], axis=0)
            east = courant[1] * jnp.take_along_axis(q, east_index, axis=2)
            west = jnp.roll(east, 1, axis=2)
            q = q - (north - south) - (east - west)
        return q

    advected = lax.map(advect, state)
    heating = advected[0] * log_thickness
    lower = jnp.cumsum(heating[:, ::-1], axis=1)[:, ::-1] - heating
    geopotential = surface[:, None, :] + lower + 0.5 * heating
    remapped = lax.map(lambda q: parabola(q, remap_level, remap_weight), advected)
    return remapped, geopotential
```

```python
import functools

import jax
import jax.numpy as jnp
from jax import lax
from jax.experimental import pallas as pl
from jax.experimental.pallas import tpu as pltpu
from jax.sharding import PartitionSpec as P

SUBSTEPS = 2


def extended_2(block, sides, width):
    for axis, dim in sides:
        count = lax.axis_size(axis)
        forward = [(i, i + 1) for i in range(count - 1)]
        backward = [(target, source) for source, target in forward]
        low = lax.ppermute(
            lax.slice_in_dim(block, block.shape[dim] - width, None, axis=dim), axis, forward
        )
        high = lax.ppermute(lax.slice_in_dim(block, 0, width, axis=dim), axis, backward)
        block = jnp.concatenate([low, block, high], axis=dim)
    return block


def from_behind(x, axis, by):
    count = lax.axis_size(axis)
    pairs = [(i, i + by) for i in range(count) if 0 <= i + by < count]
    return lax.ppermute(x, axis, pairs)


def entering(x, axis, combine, identity):
    count, position = (lax.axis_size(axis), lax.axis_index(axis))
    everything = lax.all_gather(x, axis)
    start = jnp.broadcast_to(jnp.asarray(identity, x.dtype), x.shape)

    def lap(k, before):
        at = count - 1 - k
        reached = at > position
        new = combine(before, everything[at])
        return jnp.where(reached, new, before)

    return lax.fori_loop(0, count, lap, start)


def local_parabola(extended, delta, weight):
    margin = 4
    count = extended.shape[-2] - 2 * margin
    edges = (
        7.0 * (extended[..., 1:-2, :] + extended[..., 2:-1, :])
        - (extended[..., :-3, :] + extended[..., 3:, :])
    ) / 12.0
    centre = jnp.zeros(extended.shape[:-2] + (count, extended.shape[-1]), jnp.float32)
    left = centre
    right = centre
    for offset in range(-2, 3):
        chosen = delta == offset
        start = margin + offset
        centre = jnp.where(chosen, extended[..., start : start + count, :], centre)
        left = jnp.where(chosen, edges[..., start - 2 : start - 2 + count, :], left)
        right = jnp.where(chosen, edges[..., start - 1 : start - 1 + count, :], right)
    slope = right - left
    curve = 6.0 * centre - 3.0 * (left + right)
    return left + weight * (slope + curve * (1.0 - weight))


def add_terms(earlier, later):
    return earlier + later


def per_device(state, courant, offsets, log_thickness, surface, remap_level, remap_weight):
    count, rows, levels, width = state.shape
    north_masks = [offsets[0] == offset for offset in range(-1, 3)]
    east_masks = [offsets[1] == offset for offset in range(-1, 3)]
    field = state
    for substep in range(SUBSTEPS):
        padded = extended_2(field, (("lat", 1),), 2)
        picked = jnp.zeros_like(field)
        for number, offset in enumerate(range(-1, 3)):
            picked = jnp.where(
                north_masks[number][None], padded[:, offset + 2 : offset + 2 + rows], picked
            )
        north = courant[0][None] * picked
        below = from_behind(north[:, rows - 1 :], "lat", 1)
        south = jnp.concatenate([below, north[:, : rows - 1]], axis=1)
        moved = jnp.zeros_like(field)
        for number, offset in enumerate(range(-1, 3)):
            moved = jnp.where(east_masks[number][None], jnp.roll(field, -offset, axis=3), moved)
        east = courant[1][None] * moved
        west = jnp.roll(east, 1, axis=3)
        field = field - (north - south) - (east - west)
    heating = field[0] * log_thickness
    lower = [jnp.zeros_like(heating[:, 0])]
    for level in range(levels - 1, 0, -1):
        lower.insert(0, lower[0] + heating[:, level])
    lower_local = jnp.stack(lower, axis=1)
    column_sum = jnp.sum(heating, axis=1)
    deeper = entering(column_sum, "lev", add_terms, jnp.zeros_like(column_sum))
    geopotential = surface[:, None, :] + deeper[:, None, :] + lower_local + 0.5 * heating
    total_levels = remap_level.shape[1]
    delta_col = (remap_level - jnp.arange(total_levels, dtype=jnp.int32)[None, :, None]).astype(
        jnp.float32
    )
    inputs = lax.all_to_all(
        jnp.stack([delta_col, remap_weight]), "lev", split_axis=2, concat_axis=3, tiled=True
    )
    margin = 4
    lev = lax.axis_index("lev")
    before = from_behind(field, "lev", 1)[:, :, levels - margin :]
    after = from_behind(field, "lev", -1)[:, :, :margin]
    before = jnp.where(lev == 0, field[:, :, :1], before)
    after = jnp.where(lev == lax.axis_size("lev") - 1, field[:, :, levels - 1 :], after)
    extended = jnp.concatenate([before, field, after], axis=2)
    remapped = local_parabola(extended, inputs[0][None], inputs[1][None])
    return (remapped, geopotential)


MARGIN = 4
LANES = 128
SUB = 8
LOW = 16
MESH = pl.DeviceIdType.MESH


def remote(src, dst, send, recv, axis, peer):
    return pltpu.make_async_remote_copy(
        src_ref=src,
        dst_ref=dst,
        send_sem=send,
        recv_sem=recv,
        device_id={axis: peer},
        device_id_type=MESH,
    )


def starts(count):
    return [min(at, count - SUB) for at in range(0, count, SUB)]


def copy_rows(target, to, source, at, count):
    for s in starts(count):
        target[pl.ds(to + s, SUB), :] = source[pl.ds(at + s, SUB), :]


def kernel(lats, levs, *refs):
    (
        h_state,
        h_courant,
        h_offsets,
        h_thickness,
        h_surface,
        h_level,
        h_weight,
        out,
        geo,
        state,
        courant,
        offsets,
        thickness,
        surface,
        remap_level,
        remap_weight,
        pack,
        pack_c,
        work_c,
        work,
        mid,
        norths,
        easts,
        ret,
        ext,
        rpack,
        rrecv,
        rall,
        delta,
        weight,
        thick,
        surf,
        hsum,
        psum,
        csum,
        sums,
        value,
        ins,
        fs,
        fr,
        bs,
        br,
        zs,
        zr,
        rs,
        rr,
        ps,
        pr,
        ss,
        sr,
    ) = refs
    count, rows, levels, width = state.shape
    cols = width // LANES
    band = rows * cols
    slab = band * lats
    room = work.shape[0] // count
    deep = (levels + 2 * MARGIN) * band
    piece = remap_level.shape[2]
    me = lax.axis_index("lat")
    lev = lax.axis_index("lev")
    core = lax.rem(lev, 2)
    if lats == 4:
        across = lax.rem(me + 2, lats)
        peers = [lats - 1 - me, across, lats - 1 - across]
    else:
        peers = [lax.rem(me + d, lats) for d in range(1, lats)]

    barrier = pltpu.get_barrier_semaphore()
    for d in range(1, levs):
        pl.semaphore_signal(
            barrier, inc=1, device_id={"lev": lax.rem(lev + d, levs)}, device_id_type=MESH
        )
    for peer in peers:
        pl.semaphore_signal(barrier, inc=1, device_id={"lat": peer}, device_id_type=MESH)
    loads = [
        pltpu.make_async_copy(a, b, ins.at[n])
        for n, (a, b) in enumerate(
            (
                (h_courant, courant),
                (h_offsets, offsets),
                (h_state, state),
                (h_level, remap_level),
                (h_weight, remap_weight),
                (h_thickness, thickness),
                (h_surface, surface),
            )
        )
    ]
    for c in loads:
        c.start()

    def spread(target, first, stride, tile, where):
        for c in range(cols):
            target[pl.ds(first + c, tile.shape[-2], stride=stride), :] = tile[
                (*where, slice(None), slice(c * LANES, (c + 1) * LANES))
            ]

    for c in loads[:3]:
        c.wait()
    for r in range(rows):
        for g in range(2):
            for c in range(cols):
                lanes = slice(c * LANES, (c + 1) * LANES)
                pack_c[pl.ds(g * band + r * cols + c, levels, stride=4 * band), :] = courant[
                    g, r, :, lanes
                ]
                pack_c[pl.ds((g + 2) * band + r * cols + c, levels, stride=4 * band), :] = offsets[
                    g, r, :, lanes
                ].astype(jnp.float32)
    for f in range(count):
        for r in range(rows):
            spread(pack, f * band + r * cols, count * band, state, (f, r))
    for c in loads[3:]:
        c.wait()
    for p in range(levs):
        for r in range(rows):
            lo = p * levels
            ks = lo + lax.broadcasted_iota(jnp.int32, (levels, piece), 0)
            rpack[p, 0, r] = (remap_level[r, lo : lo + levels, :] - ks).astype(jnp.float32)
            rpack[p, 1, r] = remap_weight[r, lo : lo + levels, :]
    for r in range(rows):
        spread(thick, r * cols, band, thickness, (r,))
    spread(surf, 0, cols, surface, ())
    blank = jnp.zeros((SUB, LANES), jnp.float32)
    for f in range(count):
        copy_rows(work, f * room + LOW + band * me, pack, (me * count + f) * band, band)
        for at in (*range(0, LOW, SUB), *(LOW + slab + n for n in range(0, 2 * cols, SUB))):
            work[pl.ds(f * room + at, SUB), :] = blank
    for g in range(4):
        copy_rows(work_c, g * slab + band * me, pack_c, (me * 4 + g) * band, band)
    for at in (*range(0, LOW, SUB), *(LOW + slab + n for n in range(0, 2 * cols, SUB))):
        mid[pl.ds(at, SUB), :] = blank
    for at in range(0, LOW, SUB):
        norths[pl.ds(at, SUB), :] = blank
        easts[pl.ds(at, SUB), :] = blank
    for at in range(0, SUB, SUB):
        easts[pl.ds(LOW + slab + at, SUB), :] = blank

    pl.semaphore_wait(barrier, lats + levs - 2)

    def coefficient_copy(n):
        return [
            remote(
                pack_c.at[pl.ds((peers[n] * 4 + g) * band, band)],
                work_c.at[pl.ds(g * slab + band * me, band)],
                fs.at[count + g, n],
                fr.at[count + g, n],
                "lat",
                peers[n],
            )
            for g in range(4)
        ]

    def field_copy(f, n):
        return remote(
            pack.at[pl.ds((peers[n] * count + f) * band, band)],
            work.at[pl.ds(f * room + LOW + band * me, band)],
            fs.at[f, n],
            fr.at[f, n],
            "lat",
            peers[n],
        )

    def back_copy(f, n):
        return remote(
            ret.at[pl.ds(f * slab + band * peers[n], band)],
            ext.at[pl.ds(f * deep + (MARGIN + me) * band, band)],
            bs.at[f, n],
            br.at[f, n],
            "lat",
            peers[n],
        )

    def level_copy(f, way):
        target = (0, MARGIN + levels)[way]
        source = (levels, MARGIN)[way]
        peer = (jnp.minimum(lev + 1, levs - 1), jnp.maximum(lev - 1, 0))[way]
        return remote(
            ext.at[pl.ds(f * deep + source * band, MARGIN * band)],
            ext.at[pl.ds(f * deep + target * band, MARGIN * band)],
            zs.at[f, way],
            zr.at[f, way],
            "lev",
            peer,
        )

    def remap_copy(d):
        peer = lax.rem(lev + d, levs)
        return remote(rpack.at[peer], rrecv.at[lev], rs.at[d], rr.at[d], "lev", peer)

    def pair_copy():
        return remote(hsum, psum, ps, pr, "lev", lev + 1 - 2 * core)

    def sum_copy(d):
        return remote(csum, sums.at[d], ss.at[d], sr.at[d], "lev", jnp.maximum(lev - 2 * d, core))

    ways = range(len(peers))
    for n in ways:
        for c in coefficient_copy(n):
            c.start()
    for f in range(count):
        for n in ways:
            field_copy(f, n).start()
    for d in range(1, levs):
        remap_copy(d).start()
    rrecv[lev] = rpack[lev]

    row = lax.broadcasted_iota(jnp.int32, (SUB, LANES), 0)
    lane = lax.broadcasted_iota(jnp.int32, (SUB, LANES), 1)
    last, first, two = lane == LANES - 1, lane < 1, lane < 2

    def substep(source, base, target, to):
        def q(at):
            return source[pl.ds(base + at, SUB), :]

        for p in starts(slab):
            here = q(p)
            o0, o1, c0, c1 = (
                work_c[pl.ds(g * slab + p, SUB), :] for g in (2, 3, 0, 1)
            )
            up = jnp.where(
                o0 < 0.5,
                jnp.where(o0 == 0.0, here, q(p - cols)),
                jnp.where(o0 == 1.0, q(p + cols), q(p + 2 * cols)),
            )
            norths[pl.ds(LOW + p, SUB), :] = c0 * up
            after, before = q(p + 1), q(p - 1)
            end, start = (cols - 1 - p) % cols, -p % cols
            if end < SUB:
                after = jnp.where(row == end, q(p + 1 - cols), after)
            if start < SUB:
                before = jnp.where(row == start, q(p - 1 + cols), before)
            side = jnp.where(
                o1 < 0.5,
                jnp.where(o1 == 0.0, here, pltpu.roll(jnp.where(last, before, here), 1, 1)),
                jnp.where(
                    o1 == 1.0,
                    pltpu.roll(jnp.where(first, after, here), LANES - 1, 1),
                    pltpu.roll(jnp.where(two, after, here), LANES - 2, 1),
                ),
            )
            easts[pl.ds(LOW + p, SUB), :] = c1 * side
        for p in starts(slab):
            north, south = norths[pl.ds(LOW + p, SUB), :], norths[pl.ds(LOW + p - cols, SUB), :]
            east, before = easts[pl.ds(LOW + p, SUB), :], easts[pl.ds(LOW + p - 1, SUB), :]
            start = -p % cols
            if start < SUB:
                before = jnp.where(row == start, easts[pl.ds(LOW + p - 1 + cols, SUB), :], before)
            west = pltpu.roll(jnp.where(last, before, east), 1, 1)
            target[pl.ds(to + p, SUB), :] = q(p) - (north - south) - (east - west)

    for n in ways:
        for c in coefficient_copy(n):
            c.wait_recv()

    def advect(f, carry):
        for n in ways:
            field_copy(f, n).wait_recv()
        substep(work, f * room + LOW, mid, LOW)
        substep(mid, LOW, ret, f * slab)
        for n in ways:
            back_copy(f, n).start()
        copy_rows(ext, f * deep + (MARGIN + me) * band, ret, f * slab + band * me, band)
        return carry

    lax.fori_loop(0, count, advect, 0)

    for d in range(1, levs):
        remap_copy(d).wait_recv()
    for p in range(levs):
        rall[:, :, :, p * piece : (p + 1) * piece] = rrecv[p]
    for g, target in enumerate((delta, weight)):
        for r in range(rows):
            spread(target, r * cols, band, rall, (g, r))

    def heat(k, s):
        at = ext[pl.ds((MARGIN + k) * band + s, SUB), :]
        return at * thick[pl.ds(k * band + s, SUB), :]

    def share(f, carry):
        for n in ways:
            back_copy(f, n).wait_recv()

        @pl.when(lev < levs - 1)
        def _():
            level_copy(f, 0).start()

        @pl.when(lev > 0)
        def _():
            level_copy(f, 1).start()

        return carry

    share(0, 0)
    for s in starts(band):
        hsum[pl.ds(s, SUB), :] = functools.reduce(add_terms, [heat(k, s) for k in range(levels)])
    pair_copy().start()
    share(1, 0)
    pair_copy().wait_recv()
    for s in starts(band):
        csum[pl.ds(s, SUB), :] = hsum[pl.ds(s, SUB), :] + psum[pl.ds(s, SUB), :]
    for d in range(1, levs // 2):

        @pl.when(lev >= 2 * d)
        def _():
            sum_copy(d).start()

    lax.fori_loop(2, count, share, 0)

    def remap(f, carry):
        base = f * deep

        @pl.when(lev > 0)
        def _():
            level_copy(f, 0).wait_recv()

        @pl.when(lev < levs - 1)
        def _():
            level_copy(f, 1).wait_recv()

        @pl.when(lev == 0)
        def _():
            for m in range(MARGIN):
                copy_rows(ext, base + m * band, ext, base + MARGIN * band, band)

        @pl.when(lev == levs - 1)
        def _():
            end = base + (MARGIN + levels) * band
            for m in range(MARGIN):
                copy_rows(ext, end + m * band, ext, end - band, band)

        for s in starts(band):
            q = [ext[pl.ds(base + m * band + s, SUB), :] for m in range(levels + 2 * MARGIN)]
            edge = {
                m: (7.0 * (q[m - 1] + q[m]) - (q[m - 2] + q[m + 1])) * (1.0 / 12.0)
                for m in range(2, levels + 2 * MARGIN - 1)
            }
            for k in range(levels):
                dk = delta[pl.ds(k * band + s, SUB), :]
                wk = weight[pl.ds(k * band + s, SUB), :]
                at = k + MARGIN
                centre, left, right = q[at - 2], edge[at - 2], edge[at - 1]
                for o in range(-1, 3):
                    chosen = dk == float(o)
                    centre = jnp.where(chosen, q[at + o], centre)
                    left = jnp.where(chosen, edge[at + o], left)
                    right = jnp.where(chosen, edge[at + o + 1], right)
                curve = 6.0 * centre - 3.0 * (left + right)
                value[pl.ds(k * band + s, SUB), :] = left + wk * (
                    (right - left) + curve * (1.0 - wk)
                )
        for r in range(rows):
            for c in range(cols):
                out[f, r, :, c * LANES : (c + 1) * LANES] = value[
                    pl.ds(r * cols + c, levels, stride=band), :
                ]
        return carry

    remap(0, 0)
    for d in range(1, levs // 2):

        @pl.when(lev + 2 * d < levs)
        def _():
            sum_copy(d).wait_recv()

    for s in starts(band):
        total = jnp.where(core == 0, psum[pl.ds(s, SUB), :], jnp.zeros((SUB, LANES), jnp.float32))
        for d in range(1, levs // 2):
            more = sums[d, pl.ds(s, SUB), :]
            total = total + jnp.where(lev + 2 * d < levs, more, jnp.zeros_like(more))
        below = surf[pl.ds(s, SUB), :] + total
        for k in range(levels - 1, -1, -1):
            term = heat(k, s)
            value[pl.ds(k * band + s, SUB), :] = below + 0.5 * term
            below = below + term
    for r in range(rows):
        for c in range(cols):
            geo[r, :, c * LANES : (c + 1) * LANES] = value[
                pl.ds(r * cols + c, levels, stride=band), :
            ]
    lax.fori_loop(1, count, remap, 0)

    for n in ways:
        for c in coefficient_copy(n):
            c.wait_send()
        for f in range(count):
            field_copy(f, n).wait_send()
            back_copy(f, n).wait_send()
    for d in range(1, levs):
        remap_copy(d).wait_send()
    pair_copy().wait_send()
    for f in range(count):

        @pl.when(lev < levs - 1)
        def _():
            level_copy(f, 0).wait_send()

        @pl.when(lev > 0)
        def _():
            level_copy(f, 1).wait_send()

    for d in range(1, levs // 2):

        @pl.when(lev >= 2 * d)
        def _():
            sum_copy(d).wait_send()


def fused(lats, levs, *args):
    state, courant, offsets, thickness, surface, level, weight = args
    count, rows, levels, width = state.shape
    piece = level.shape[2]
    cols = width // LANES
    band = rows * cols
    slab = band * lats
    room = LOW + slab + -(-2 * cols // SUB) * SUB
    room = -(-room // SUB) * SUB
    f32 = jnp.float32
    dma = pltpu.SemaphoreType.DMA

    def tall(n):
        return pltpu.VMEM((-(-n // SUB) * SUB, LANES), f32)

    return pl.pallas_call(
        functools.partial(kernel, lats, levs),
        out_shape=(pltpu.VMEM(state.shape, f32), pltpu.VMEM(thickness.shape, f32)),
        in_specs=[pl.BlockSpec(memory_space=pl.ANY)] * 7,
        scratch_shapes=[
            *(pltpu.VMEM(x.shape, x.dtype) for x in args),
            tall(levels * count * band),
            tall(levels * 4 * band),
            tall(4 * slab),
            tall(count * room),
            tall(room),
            tall(LOW + slab),
            tall(LOW + slab + SUB),
            tall(count * slab),
            tall(count * (levels + 2 * MARGIN) * band),
            pltpu.VMEM((levs, 2, rows, levels, piece), f32),
            pltpu.VMEM((levs, 2, rows, levels, piece), f32),
            pltpu.VMEM((2, rows, levels, width), f32),
            tall(levels * band),
            tall(levels * band),
            tall(levels * band),
            tall(band),
            tall(band),
            tall(band),
            tall(band),
            pltpu.VMEM((levs // 2, -(-band // SUB) * SUB, LANES), f32),
            tall(levels * band),
            dma((7,)),
            dma((count + 4, lats)),
            dma((count + 4, lats)),
            dma((count, lats)),
            dma((count, lats)),
            dma((count, 2)),
            dma((count, 2)),
            dma((levs,)),
            dma((levs,)),
            dma,
            dma,
            dma((levs // 2,)),
            dma((levs // 2,)),
        ],
        compiler_params=pltpu.CompilerParams(collective_id=0, has_side_effects=True),
    )(*args)


def solution(mesh):
    in_specs = (
        P(None, "lat", "lev", None),
        P(None, "lat", "lev", None),
        P(None, "lat", "lev", None),
        P("lat", "lev", None),
        P("lat", None),
        P("lat", None, "lev"),
        P("lat", None, "lev"),
    )
    out_specs = (P(None, "lat", "lev", None), P("lat", "lev", None))
    lats, levs = mesh.shape["lat"], mesh.shape["lev"]

    def body(state, *rest):
        count, rows, levels, width = state.shape
        small = width % LANES or rows * (width // LANES) < SUB or LOW < width // LANES
        if levels != lats or levels != MARGIN or small or levs % 2 or count < 2:
            return per_device(state, *rest)
        return fused(lats, levs, state, *rest)

    return jax.shard_map(
        body, mesh=mesh, in_specs=in_specs, out_specs=out_specs, check_vma=False
    )
```

```python
import functools

import jax
import jax.numpy as jnp
from jax import lax
from jax.experimental import pallas as pl
from jax.experimental.pallas import tpu as pltpu
from jax.sharding import PartitionSpec as P

SUBSTEPS = 2


def extended_2(block, sides, width):
    for axis, dim in sides:
        count = lax.axis_size(axis)
        forward = [(i, i + 1) for i in range(count - 1)]
        backward = [(target, source) for source, target in forward]
        low = lax.ppermute(
            lax.slice_in_dim(block, block.shape[dim] - width, None, axis=dim), axis, forward
        )
        high = lax.ppermute(lax.slice_in_dim(block, 0, width, axis=dim), axis, backward)
        block = jnp.concatenate([low, block, high], axis=dim)
    return block


def from_behind(x, axis, by):
    count = lax.axis_size(axis)
    pairs = [(i, i + by) for i in range(count) if 0 <= i + by < count]
    return lax.ppermute(x, axis, pairs)


def entering(x, axis, combine, identity):
    count, position = (lax.axis_size(axis), lax.axis_index(axis))
    everything = lax.all_gather(x, axis)
    start = jnp.broadcast_to(jnp.asarray(identity, x.dtype), x.shape)

    def lap(k, before):
        at = count - 1 - k
        reached = at > position
        new = combine(before, everything[at])
        return jnp.where(reached, new, before)

    return lax.fori_loop(0, count, lap, start)


def local_parabola(extended, delta, weight):
    margin = 4
    count = extended.shape[-2] - 2 * margin
    edges = (
        7.0 * (extended[..., 1:-2, :] + extended[..., 2:-1, :])
        - (extended[..., :-3, :] + extended[..., 3:, :])
    ) / 12.0
    centre = jnp.zeros(extended.shape[:-2] + (count, extended.shape[-1]), jnp.float32)
    left = centre
    right = centre
    for offset in range(-2, 3):
        chosen = delta == offset
        start = margin + offset
        centre = jnp.where(chosen, extended[..., start : start + count, :], centre)
        left = jnp.where(chosen, edges[..., start - 2 : start - 2 + count, :], left)
        right = jnp.where(chosen, edges[..., start - 1 : start - 1 + count, :], right)
    slope = right - left
    curve = 6.0 * centre - 3.0 * (left + right)
    return left + weight * (slope + curve * (1.0 - weight))


def add_terms(earlier, later):
    return earlier + later


def per_device(state, courant, offsets, log_thickness, surface, remap_level, remap_weight):
    count, rows, levels, width = state.shape
    north_masks = [offsets[0] == offset for offset in range(-1, 3)]
    east_masks = [offsets[1] == offset for offset in range(-1, 3)]
    field = state
    for substep in range(SUBSTEPS):
        padded = extended_2(field, (("lat", 1),), 2)
        picked = jnp.zeros_like(field)
        for number, offset in enumerate(range(-1, 3)):
            picked = jnp.where(
                north_masks[number][None], padded[:, offset + 2 : offset + 2 + rows], picked
            )
        north = courant[0][None] * picked
        below = from_behind(north[:, rows - 1 :], "lat", 1)
        south = jnp.concatenate([below, north[:, : rows - 1]], axis=1)
        moved = jnp.zeros_like(field)
        for number, offset in enumerate(range(-1, 3)):
            moved = jnp.where(east_masks[number][None], jnp.roll(field, -offset, axis=3), moved)
        east = courant[1][None] * moved
        west = jnp.roll(east, 1, axis=3)
        field = field - (north - south) - (east - west)
    heating = field[0] * log_thickness
    lower = [jnp.zeros_like(heating[:, 0])]
    for level in range(levels - 1, 0, -1):
        lower.insert(0, lower[0] + heating[:, level])
    lower_local = jnp.stack(lower, axis=1)
    column_sum = jnp.sum(heating, axis=1)
    deeper = entering(column_sum, "lev", add_terms, jnp.zeros_like(column_sum))
    geopotential = surface[:, None, :] + deeper[:, None, :] + lower_local + 0.5 * heating
    total_levels = remap_level.shape[1]
    delta_col = (remap_level - jnp.arange(total_levels, dtype=jnp.int32)[None, :, None]).astype(
        jnp.float32
    )
    inputs = lax.all_to_all(
        jnp.stack([delta_col, remap_weight]), "lev", split_axis=2, concat_axis=3, tiled=True
    )
    margin = 4
    lev = lax.axis_index("lev")
    before = from_behind(field, "lev", 1)[:, :, levels - margin :]
    after = from_behind(field, "lev", -1)[:, :, :margin]
    before = jnp.where(lev == 0, field[:, :, :1], before)
    after = jnp.where(lev == lax.axis_size("lev") - 1, field[:, :, levels - 1 :], after)
    extended = jnp.concatenate([before, field, after], axis=2)
    remapped = local_parabola(extended, inputs[0][None], inputs[1][None])
    return (remapped, geopotential)


MARGIN = 4
LANES = 128
SUB = 8
LOW = 16
MESH = pl.DeviceIdType.MESH


def remote(src, dst, send, recv, axis, peer):
    return pltpu.make_async_remote_copy(
        src_ref=src,
        dst_ref=dst,
        send_sem=send,
        recv_sem=recv,
        device_id={axis: peer},
        device_id_type=MESH,
    )


def starts(count):
    return [min(at, count - SUB) for at in range(0, count, SUB)]


def copy_rows(target, to, source, at, count):
    for s in starts(count):
        target[pl.ds(to + s, SUB), :] = source[pl.ds(at + s, SUB), :]


def kernel(lats, levs, *refs):
    (
        h_state,
        h_courant,
        h_offsets,
        h_thickness,
        h_surface,
        h_level,
        h_weight,
        out,
        geo,
        state,
        courant,
        offsets,
        thickness,
        surface,
        remap_level,
        remap_weight,
        pack,
        pack_c,
        work_c,
        work,
        mid,
        norths,
        easts,
        ret,
        ext,
        rpack,
        rrecv,
        rall,
        delta,
        weight,
        thick,
        surf,
        hsum,
        psum,
        csum,
        sums,
        below_all,
        value,
        ins,
        fs,
        fr,
        bs,
        br,
        zs,
        zr,
        rs,
        rr,
        ps,
        pr,
        ss,
        sr,
        ts,
        tr,
        far,
    ) = refs
    count, rows, levels, width = state.shape
    cols = width // LANES
    band = rows * cols
    slab = band * lats
    room = work.shape[0] // count
    deep = (levels + 2 * MARGIN) * band
    piece = remap_level.shape[2]
    me = lax.axis_index("lat")
    lev = lax.axis_index("lev")
    core = lax.rem(lev, 2)
    if lats == 4:
        across = lax.rem(me + 2, lats)
        peers = [lats - 1 - me, across, lats - 1 - across]
    else:
        peers = [lax.rem(me + d, lats) for d in range(1, lats)]

    barrier = pltpu.get_barrier_semaphore()
    chips = levs // 2
    chip = lev // 2
    for peer in peers:
        pl.semaphore_signal(barrier, inc=1, device_id={"lat": peer}, device_id_type=MESH)
    pl.semaphore_signal(
        barrier, inc=1, device_id={"lev": lev + 1 - 2 * core}, device_id_type=MESH
    )

    def near(step):
        return jnp.logical_and(chip + step >= 0, chip + step < chips)

    for step in (-1, 1):
        for c in range(2):

            @pl.when(near(step))
            def _():
                pl.semaphore_signal(
                    barrier,
                    inc=1,
                    device_id={"lev": jnp.clip(2 * (chip + step) + c, 0, levs - 1)},
                    device_id_type=MESH,
                )

    loads = [
        pltpu.make_async_copy(a, b, ins.at[n])
        for n, (a, b) in enumerate(
            (
                (h_courant, courant),
                (h_offsets, offsets),
                (h_state, state),
                (h_level, remap_level),
                (h_weight, remap_weight),
                (h_thickness, thickness),
                (h_surface, surface),
            )
        )
    ]
    for c in loads:
        c.start()

    def spread(target, first, stride, tile, where):
        for c in range(cols):
            target[pl.ds(first + c, tile.shape[-2], stride=stride), :] = tile[
                (*where, slice(None), slice(c * LANES, (c + 1) * LANES))
            ]

    for c in loads[:3]:
        c.wait()
    for r in range(rows):
        for g in range(2):
            for c in range(cols):
                lanes = slice(c * LANES, (c + 1) * LANES)
                pack_c[pl.ds(g * band + r * cols + c, levels, stride=4 * band), :] = courant[
                    g, r, :, lanes
                ]
                pack_c[pl.ds((g + 2) * band + r * cols + c, levels, stride=4 * band), :] = offsets[
                    g, r, :, lanes
                ].astype(jnp.float32)
    for f in range(count):
        for r in range(rows):
            spread(pack, f * band + r * cols, count * band, state, (f, r))
    for c in loads[3:]:
        c.wait()
    for p in range(levs):
        for r in range(rows):
            lo = p * levels
            ks = lo + lax.broadcasted_iota(jnp.int32, (levels, piece), 0)
            rpack[p, 0, r] = (remap_level[r, lo : lo + levels, :] - ks).astype(jnp.float32)
            rpack[p, 1, r] = remap_weight[r, lo : lo + levels, :]
    for r in range(rows):
        spread(thick, r * cols, band, thickness, (r,))
    spread(surf, 0, cols, surface, ())
    blank = jnp.zeros((SUB, LANES), jnp.float32)
    for f in range(count):
        copy_rows(work, f * room + LOW + band * me, pack, (me * count + f) * band, band)
        for at in (*range(0, LOW, SUB), *(LOW + slab + n for n in range(0, 2 * cols, SUB))):
            work[pl.ds(f * room + at, SUB), :] = blank
    for g in range(4):
        copy_rows(work_c, g * slab + band * me, pack_c, (me * 4 + g) * band, band)
    for at in (*range(0, LOW, SUB), *(LOW + slab + n for n in range(0, 2 * cols, SUB))):
        mid[pl.ds(at, SUB), :] = blank
    for at in range(0, LOW, SUB):
        norths[pl.ds(at, SUB), :] = blank
        easts[pl.ds(at, SUB), :] = blank
    for at in range(0, SUB, SUB):
        easts[pl.ds(LOW + slab + at, SUB), :] = blank

    sides = (chip > 0).astype(jnp.int32) + (chip < chips - 1).astype(jnp.int32)
    pl.semaphore_wait(barrier, len(peers) + 1 + 2 * sides)

    def coefficient_copy(n):
        return [
            remote(
                pack_c.at[pl.ds((peers[n] * 4 + g) * band, band)],
                work_c.at[pl.ds(g * slab + band * me, band)],
                fs.at[count + g, n],
                fr.at[count + g, n],
                "lat",
                peers[n],
            )
            for g in range(4)
        ]

    def field_copy(f, n):
        return remote(
            pack.at[pl.ds((peers[n] * count + f) * band, band)],
            work.at[pl.ds(f * room + LOW + band * me, band)],
            fs.at[f, n],
            fr.at[f, n],
            "lat",
            peers[n],
        )

    def back_copy(f, n):
        return remote(
            ret.at[pl.ds(f * slab + band * peers[n], band)],
            ext.at[pl.ds(f * deep + (MARGIN + me) * band, band)],
            bs.at[f, n],
            br.at[f, n],
            "lat",
            peers[n],
        )

    def level_copy(f, way):
        target = (0, MARGIN + levels)[way]
        source = (levels, MARGIN)[way]
        peer = (jnp.minimum(lev + 1, levs - 1), jnp.maximum(lev - 1, 0))[way]
        return remote(
            ext.at[pl.ds(f * deep + source * band, MARGIN * band)],
            ext.at[pl.ds(f * deep + target * band, MARGIN * band)],
            zs.at[f, way],
            zr.at[f, way],
            "lev",
            peer,
        )

    def spread_remap(step):
        for c in range(2):
            if step or c:

                @pl.when(near(step))
                def _():
                    remap_copy(step, c).start()

    def remap_copy(step, c):
        n = chips - 1 + step
        to = jnp.clip(2 * (chip + step) + (c + core) % 2, 0, levs - 1)
        return remote(rpack.at[to], rrecv.at[lev], rs.at[n, c], rr.at[n, c], "lev", to)

    def remap_arrival(step, c):
        n = chips - 1 + step
        return remote(
            rpack.at[lev], rrecv.at[lev], rs.at[n, c], rr.at[n, c], "lev", lev + 1 - 2 * core
        )

    def relay(way, hop):
        step = (1, -1)[way]

        @pl.when(jnp.logical_and(near(step), near(-step * hop)))
        def _():
            pl.semaphore_signal(
                far.at[way, hop],
                inc=1,
                device_id={"lev": jnp.clip(lev + 2 * step, 0, levs - 1)},
                device_id_type=MESH,
            )

    def pair_copy():
        return remote(hsum, psum, ps, pr, "lev", lev + 1 - 2 * core)

    def sum_copy(d):
        return remote(csum, sums.at[d], ss.at[d], sr.at[d], "lev", jnp.maximum(lev - 2 * d, core))

    def total_copy():
        return remote(below_all, below_all, ts, tr, "lev", lev + 1 - 2 * core)

    ways = range(len(peers))
    for way in range(2):
        relay(way, 1)
    for n in ways:
        for c in coefficient_copy(n):
            c.start()
    for f in range(count):
        for n in ways:
            field_copy(f, n).start()
    rrecv[lev] = rpack[lev]
    for step in (-1, 0, 1):
        spread_remap(step)
    for hop in range(1, chips - 1):
        for way in range(2):
            back = -(hop + 1) if way == 0 else hop + 1

            @pl.when(near(back))
            def _():
                pl.semaphore_wait(far.at[way, hop], 1)

            if hop + 1 < chips - 1:
                relay(way, hop + 1)
            spread_remap(back)

    row = lax.broadcasted_iota(jnp.int32, (SUB, LANES), 0)
    lane = lax.broadcasted_iota(jnp.int32, (SUB, LANES), 1)
    last, first, two = lane == LANES - 1, lane < 1, lane < 2

    def substep(source, base, target, to):
        def q(at):
            return source[pl.ds(base + at, SUB), :]

        for p in starts(slab):
            here = q(p)
            o0, o1, c0, c1 = (
                work_c[pl.ds(g * slab + p, SUB), :] for g in (2, 3, 0, 1)
            )
            up = jnp.where(
                o0 < 0.5,
                jnp.where(o0 == 0.0, here, q(p - cols)),
                jnp.where(o0 == 1.0, q(p + cols), q(p + 2 * cols)),
            )
            norths[pl.ds(LOW + p, SUB), :] = c0 * up
            after, before = q(p + 1), q(p - 1)
            end, start = (cols - 1 - p) % cols, -p % cols
            if end < SUB:
                after = jnp.where(row == end, q(p + 1 - cols), after)
            if start < SUB:
                before = jnp.where(row == start, q(p - 1 + cols), before)
            side = jnp.where(
                o1 < 0.5,
                jnp.where(o1 == 0.0, here, pltpu.roll(jnp.where(last, before, here), 1, 1)),
                jnp.where(
                    o1 == 1.0,
                    pltpu.roll(jnp.where(first, after, here), LANES - 1, 1),
                    pltpu.roll(jnp.where(two, after, here), LANES - 2, 1),
                ),
            )
            easts[pl.ds(LOW + p, SUB), :] = c1 * side
        for p in starts(slab):
            north, south = norths[pl.ds(LOW + p, SUB), :], norths[pl.ds(LOW + p - cols, SUB), :]
            east, before = easts[pl.ds(LOW + p, SUB), :], easts[pl.ds(LOW + p - 1, SUB), :]
            start = -p % cols
            if start < SUB:
                before = jnp.where(row == start, easts[pl.ds(LOW + p - 1 + cols, SUB), :], before)
            west = pltpu.roll(jnp.where(last, before, east), 1, 1)
            target[pl.ds(to + p, SUB), :] = q(p) - (north - south) - (east - west)

    for n in ways:
        for c in coefficient_copy(n):
            c.wait_recv()

    def advect(f, carry):
        for n in ways:
            field_copy(f, n).wait_recv()
        substep(work, f * room + LOW, mid, LOW)
        substep(mid, LOW, ret, f * slab)
        for n in ways:
            back_copy(f, n).start()
        copy_rows(ext, f * deep + (MARGIN + me) * band, ret, f * slab + band * me, band)
        return carry

    lax.fori_loop(0, count, advect, 0)

    for n in ways:
        for c in coefficient_copy(n):
            c.wait_send()
        for f in range(count):
            field_copy(f, n).wait_send()
    for step in range(1 - chips, chips):
        for c in range(2):
            if step or c:

                @pl.when(near(-step))
                def _():
                    remap_arrival(step, c).wait_recv()

                @pl.when(near(step))
                def _():
                    remap_copy(step, c).wait_send()

    for p in range(levs):
        rall[:, :, :, p * piece : (p + 1) * piece] = rrecv[p]
    for g, target in enumerate((delta, weight)):
        for r in range(rows):
            spread(target, r * cols, band, rall, (g, r))

    def heat(k, s):
        at = ext[pl.ds((MARGIN + k) * band + s, SUB), :]
        return at * thick[pl.ds(k * band + s, SUB), :]

    def level_start(f):
        @pl.when(lev < levs - 1)
        def _():
            level_copy(f, 0).start()

        @pl.when(lev > 0)
        def _():
            level_copy(f, 1).start()

    def share(f, carry):
        for n in ways:
            back_copy(f, n).wait_recv()
        level_start(f)
        for n in ways:
            back_copy(f, n).wait_send()
        return carry

    for n in ways:
        back_copy(0, n).wait_recv()
    for s in starts(band):
        hsum[pl.ds(s, SUB), :] = functools.reduce(add_terms, [heat(k, s) for k in range(levels)])
    pair_copy().start()
    level_start(0)
    pair_copy().wait_recv()
    for s in starts(band):
        csum[pl.ds(s, SUB), :] = hsum[pl.ds(s, SUB), :] + psum[pl.ds(s, SUB), :]
    for d in range(1, levs // 2):

        @pl.when(jnp.logical_and(core == 0, lev >= 2 * d))
        def _():
            sum_copy(d).start()

    lax.fori_loop(1, count, share, 0)

    def remap(f, carry):
        base = f * deep

        @pl.when(lev > 0)
        def _():
            level_copy(f, 0).wait_recv()
            level_copy(f, 1).wait_send()

        @pl.when(lev < levs - 1)
        def _():
            level_copy(f, 1).wait_recv()
            level_copy(f, 0).wait_send()

        @pl.when(lev == 0)
        def _():
            for m in range(MARGIN):
                copy_rows(ext, base + m * band, ext, base + MARGIN * band, band)

        @pl.when(lev == levs - 1)
        def _():
            end = base + (MARGIN + levels) * band
            for m in range(MARGIN):
                copy_rows(ext, end + m * band, ext, end - band, band)

        for s in starts(band):
            q = [ext[pl.ds(base + m * band + s, SUB), :] for m in range(levels + 2 * MARGIN)]
            edge = {
                m: (7.0 * (q[m - 1] + q[m]) - (q[m - 2] + q[m + 1])) * (1.0 / 12.0)
                for m in range(2, levels + 2 * MARGIN - 1)
            }
            for k in range(levels):
                dk = delta[pl.ds(k * band + s, SUB), :]
                wk = weight[pl.ds(k * band + s, SUB), :]
                at = k + MARGIN
                centre, left, right = q[at - 2], edge[at - 2], edge[at - 1]
                for o in range(-1, 3):
                    chosen = dk == float(o)
                    centre = jnp.where(chosen, q[at + o], centre)
                    left = jnp.where(chosen, edge[at + o], left)
                    right = jnp.where(chosen, edge[at + o + 1], right)
                curve = 6.0 * centre - 3.0 * (left + right)
                value[pl.ds(k * band + s, SUB), :] = left + wk * (
                    (right - left) + curve * (1.0 - wk)
                )
        for r in range(rows):
            for c in range(cols):
                out[f, r, :, c * LANES : (c + 1) * LANES] = value[
                    pl.ds(r * cols + c, levels, stride=band), :
                ]
        return carry

    lax.fori_loop(0, count - 1, remap, 0)
    @pl.when(core == 0)
    def _():
        for d in range(1, chips):

            @pl.when(chip + d < chips)
            def _():
                sum_copy(d).wait_recv()

        for s in starts(band):
            total = jnp.zeros((SUB, LANES), jnp.float32)
            for d in range(1, chips):
                more = sums[d, pl.ds(s, SUB), :]
                total = total + jnp.where(chip + d < chips, more, jnp.zeros_like(more))
            below_all[pl.ds(s, SUB), :] = total
        total_copy().start()

    remap(count - 1, 0)

    @pl.when(core == 1)
    def _():
        total_copy().wait_recv()

    for s in starts(band):
        pair = psum[pl.ds(s, SUB), :]
        below = surf[pl.ds(s, SUB), :] + below_all[pl.ds(s, SUB), :]
        below = below + jnp.where(core == 0, pair, jnp.zeros_like(pair))
        for k in range(levels - 1, -1, -1):
            term = heat(k, s)
            value[pl.ds(k * band + s, SUB), :] = below + 0.5 * term
            below = below + term
    for r in range(rows):
        for c in range(cols):
            geo[r, :, c * LANES : (c + 1) * LANES] = value[
                pl.ds(r * cols + c, levels, stride=band), :
            ]

    for n in ways:
        back_copy(0, n).wait_send()
    pair_copy().wait_send()

    @pl.when(core == 0)
    def _():
        total_copy().wait_send()
        for d in range(1, chips):

            @pl.when(lev >= 2 * d)
            def _():
                sum_copy(d).wait_send()


def fused(lats, levs, *args):
    state, courant, offsets, thickness, surface, level, weight = args
    count, rows, levels, width = state.shape
    piece = level.shape[2]
    cols = width // LANES
    band = rows * cols
    slab = band * lats
    room = LOW + slab + -(-2 * cols // SUB) * SUB
    room = -(-room // SUB) * SUB
    f32 = jnp.float32
    dma = pltpu.SemaphoreType.DMA

    def tall(n):
        return pltpu.VMEM((-(-n // SUB) * SUB, LANES), f32)

    return pl.pallas_call(
        functools.partial(kernel, lats, levs),
        out_shape=(pltpu.VMEM(state.shape, f32), pltpu.VMEM(thickness.shape, f32)),
        in_specs=[pl.BlockSpec(memory_space=pl.ANY)] * 7,
        scratch_shapes=[
            *(pltpu.VMEM(x.shape, x.dtype) for x in args),
            tall(levels * count * band),
            tall(levels * 4 * band),
            tall(4 * slab),
            tall(count * room),
            tall(room),
            tall(LOW + slab),
            tall(LOW + slab + SUB),
            tall(count * slab),
            tall(count * (levels + 2 * MARGIN) * band),
            pltpu.VMEM((levs, 2, rows, levels, piece), f32),
            pltpu.VMEM((levs, 2, rows, levels, piece), f32),
            pltpu.VMEM((2, rows, levels, width), f32),
            tall(levels * band),
            tall(levels * band),
            tall(levels * band),
            tall(band),
            tall(band),
            tall(band),
            tall(band),
            pltpu.VMEM((levs // 2, -(-band // SUB) * SUB, LANES), f32),
            tall(band),
            tall(levels * band),
            dma((7,)),
            dma((count + 4, lats)),
            dma((count + 4, lats)),
            dma((count, lats)),
            dma((count, lats)),
            dma((count, 2)),
            dma((count, 2)),
            dma((levs, 2)),
            dma((levs, 2)),
            dma,
            dma,
            dma((levs // 2,)),
            dma((levs // 2,)),
            dma,
            dma,
            pltpu.SemaphoreType.REGULAR((2, levs // 2)),
        ],
        compiler_params=pltpu.CompilerParams(collective_id=0, has_side_effects=True),
    )(*args)


def solution(mesh):
    in_specs = (
        P(None, "lat", "lev", None),
        P(None, "lat", "lev", None),
        P(None, "lat", "lev", None),
        P("lat", "lev", None),
        P("lat", None),
        P("lat", None, "lev"),
        P("lat", None, "lev"),
    )
    out_specs = (P(None, "lat", "lev", None), P("lat", "lev", None))
    lats, levs = mesh.shape["lat"], mesh.shape["lev"]

    def body(state, *rest):
        count, rows, levels, width = state.shape
        small = width % LANES or rows * (width // LANES) < SUB or LOW < width // LANES
        if levels != lats or levels != MARGIN or small or levs % 2 or count < 2:
            return per_device(state, *rest)
        return fused(lats, levs, state, *rest)

    return jax.shard_map(
        body, mesh=mesh, in_specs=in_specs, out_specs=out_specs, check_vma=False
    )
```

```python
import functools

import jax
import jax.numpy as jnp
from jax import lax
from jax.experimental import pallas as pl
from jax.experimental.pallas import tpu as pltpu
from jax.sharding import PartitionSpec as P

SUBSTEPS = 2


def extended_2(block, sides, width):
    for axis, dim in sides:
        count = lax.axis_size(axis)
        forward = [(i, i + 1) for i in range(count - 1)]
        backward = [(target, source) for source, target in forward]
        low = lax.ppermute(
            lax.slice_in_dim(block, block.shape[dim] - width, None, axis=dim), axis, forward
        )
        high = lax.ppermute(lax.slice_in_dim(block, 0, width, axis=dim), axis, backward)
        block = jnp.concatenate([low, block, high], axis=dim)
    return block


def from_behind(x, axis, by):
    count = lax.axis_size(axis)
    pairs = [(i, i + by) for i in range(count) if 0 <= i + by < count]
    return lax.ppermute(x, axis, pairs)


def entering(x, axis, combine, identity):
    count, position = (lax.axis_size(axis), lax.axis_index(axis))
    everything = lax.all_gather(x, axis)
    start = jnp.broadcast_to(jnp.asarray(identity, x.dtype), x.shape)

    def lap(k, before):
        at = count - 1 - k
        reached = at > position
        new = combine(before, everything[at])
        return jnp.where(reached, new, before)

    return lax.fori_loop(0, count, lap, start)


def local_parabola(extended, delta, weight):
    margin = 4
    count = extended.shape[-2] - 2 * margin
    edges = (
        7.0 * (extended[..., 1:-2, :] + extended[..., 2:-1, :])
        - (extended[..., :-3, :] + extended[..., 3:, :])
    ) / 12.0
    centre = jnp.zeros(extended.shape[:-2] + (count, extended.shape[-1]), jnp.float32)
    left = centre
    right = centre
    for offset in range(-2, 3):
        chosen = delta == offset
        start = margin + offset
        centre = jnp.where(chosen, extended[..., start : start + count, :], centre)
        left = jnp.where(chosen, edges[..., start - 2 : start - 2 + count, :], left)
        right = jnp.where(chosen, edges[..., start - 1 : start - 1 + count, :], right)
    slope = right - left
    curve = 6.0 * centre - 3.0 * (left + right)
    return left + weight * (slope + curve * (1.0 - weight))


def add_terms(earlier, later):
    return earlier + later


def per_device(state, courant, offsets, log_thickness, surface, remap_level, remap_weight):
    count, rows, levels, width = state.shape
    north_masks = [offsets[0] == offset for offset in range(-1, 3)]
    east_masks = [offsets[1] == offset for offset in range(-1, 3)]
    field = state
    for substep in range(SUBSTEPS):
        padded = extended_2(field, (("lat", 1),), 2)
        picked = jnp.zeros_like(field)
        for number, offset in enumerate(range(-1, 3)):
            picked = jnp.where(
                north_masks[number][None], padded[:, offset + 2 : offset + 2 + rows], picked
            )
        north = courant[0][None] * picked
        below = from_behind(north[:, rows - 1 :], "lat", 1)
        south = jnp.concatenate([below, north[:, : rows - 1]], axis=1)
        moved = jnp.zeros_like(field)
        for number, offset in enumerate(range(-1, 3)):
            moved = jnp.where(east_masks[number][None], jnp.roll(field, -offset, axis=3), moved)
        east = courant[1][None] * moved
        west = jnp.roll(east, 1, axis=3)
        field = field - (north - south) - (east - west)
    heating = field[0] * log_thickness
    lower = [jnp.zeros_like(heating[:, 0])]
    for level in range(levels - 1, 0, -1):
        lower.insert(0, lower[0] + heating[:, level])
    lower_local = jnp.stack(lower, axis=1)
    column_sum = jnp.sum(heating, axis=1)
    deeper = entering(column_sum, "lev", add_terms, jnp.zeros_like(column_sum))
    geopotential = surface[:, None, :] + deeper[:, None, :] + lower_local + 0.5 * heating
    total_levels = remap_level.shape[1]
    delta_col = (remap_level - jnp.arange(total_levels, dtype=jnp.int32)[None, :, None]).astype(
        jnp.float32
    )
    inputs = lax.all_to_all(
        jnp.stack([delta_col, remap_weight]), "lev", split_axis=2, concat_axis=3, tiled=True
    )
    margin = 4
    lev = lax.axis_index("lev")
    before = from_behind(field, "lev", 1)[:, :, levels - margin :]
    after = from_behind(field, "lev", -1)[:, :, :margin]
    before = jnp.where(lev == 0, field[:, :, :1], before)
    after = jnp.where(lev == lax.axis_size("lev") - 1, field[:, :, levels - 1 :], after)
    extended = jnp.concatenate([before, field, after], axis=2)
    remapped = local_parabola(extended, inputs[0][None], inputs[1][None])
    return (remapped, geopotential)


MARGIN = 4
LANES = 128
SUB = 8
LOW = 16
MESH = pl.DeviceIdType.MESH


def remote(src, dst, send, recv, axis, peer):
    return pltpu.make_async_remote_copy(
        src_ref=src,
        dst_ref=dst,
        send_sem=send,
        recv_sem=recv,
        device_id={axis: peer},
        device_id_type=MESH,
    )


def starts(count):
    return [min(at, count - SUB) for at in range(0, count, SUB)]


def copy_rows(target, to, source, at, count):
    for s in starts(count):
        target[pl.ds(to + s, SUB), :] = source[pl.ds(at + s, SUB), :]


def kernel(lats, levs, *refs):
    (
        h_state,
        h_courant,
        h_offsets,
        h_thickness,
        h_surface,
        h_level,
        h_weight,
        out,
        geo,
        state,
        courant,
        offsets,
        thickness,
        surface,
        remap_level,
        remap_weight,
        pack,
        pack_c,
        work_c,
        work,
        mid,
        norths,
        easts,
        ret,
        ext,
        rpack,
        rrecv,
        rall,
        delta,
        weight,
        thick,
        surf,
        hsum,
        psum,
        csum,
        sums,
        below_all,
        value,
        ins,
        fs,
        fr,
        bs,
        br,
        zs,
        zr,
        rs,
        rr,
        ps,
        pr,
        ss,
        sr,
        ts,
        tr,
        far,
    ) = refs
    count, rows, levels, width = state.shape
    cols = width // LANES
    band = rows * cols
    slab = band * lats
    room = work.shape[0] // count
    deep = (levels + 2 * MARGIN) * band
    piece = remap_level.shape[2]
    me = lax.axis_index("lat")
    lev = lax.axis_index("lev")
    core = lax.rem(lev, 2)
    if lats == 4:
        across = lax.rem(me + 2, lats)
        peers = [lats - 1 - me, across, lats - 1 - across]
    else:
        peers = [lax.rem(me + d, lats) for d in range(1, lats)]

    barrier = pltpu.get_barrier_semaphore()
    chips = levs // 2
    chip = lev // 2
    for peer in peers:
        pl.semaphore_signal(barrier, inc=1, device_id={"lat": peer}, device_id_type=MESH)
    pl.semaphore_signal(
        barrier, inc=1, device_id={"lev": lev + 1 - 2 * core}, device_id_type=MESH
    )

    def near(step):
        return jnp.logical_and(chip + step >= 0, chip + step < chips)

    for step in (-1, 1):
        for c in range(2):

            @pl.when(near(step))
            def _():
                pl.semaphore_signal(
                    barrier,
                    inc=1,
                    device_id={"lev": jnp.clip(2 * (chip + step) + c, 0, levs - 1)},
                    device_id_type=MESH,
                )

    loads = [
        pltpu.make_async_copy(a, b, ins.at[n])
        for n, (a, b) in enumerate(
            (
                (h_courant, courant),
                (h_offsets, offsets),
                (h_state, state),
                (h_level, remap_level),
                (h_weight, remap_weight),
                (h_thickness, thickness),
                (h_surface, surface),
            )
        )
    ]
    for c in loads:
        c.start()

    def spread(target, first, stride, tile, where):
        for c in range(cols):
            target[pl.ds(first + c, tile.shape[-2], stride=stride), :] = tile[
                (*where, slice(None), slice(c * LANES, (c + 1) * LANES))
            ]

    for c in loads[:3]:
        c.wait()
    for r in range(rows):
        for g in range(2):
            for c in range(cols):
                lanes = slice(c * LANES, (c + 1) * LANES)
                pack_c[pl.ds(g * band + r * cols + c, levels, stride=4 * band), :] = courant[
                    g, r, :, lanes
                ]
                pack_c[pl.ds((g + 2) * band + r * cols + c, levels, stride=4 * band), :] = offsets[
                    g, r, :, lanes
                ].astype(jnp.float32)
    for f in range(count):
        for r in range(rows):
            spread(pack, f * band + r * cols, count * band, state, (f, r))

    sides = (chip > 0).astype(jnp.int32) + (chip < chips - 1).astype(jnp.int32)
    pl.semaphore_wait(barrier, len(peers) + 1 + 2 * sides)

    def coefficient_copy(n):
        return [
            remote(
                pack_c.at[pl.ds((peers[n] * 4 + g) * band, band)],
                work_c.at[pl.ds(g * slab + band * me, band)],
                fs.at[count + g, n],
                fr.at[count + g, n],
                "lat",
                peers[n],
            )
            for g in range(4)
        ]

    def field_copy(f, n):
        return remote(
            pack.at[pl.ds((peers[n] * count + f) * band, band)],
            work.at[pl.ds(f * room + LOW + band * me, band)],
            fs.at[f, n],
            fr.at[f, n],
            "lat",
            peers[n],
        )

    def back_copy(f, n):
        return remote(
            ret.at[pl.ds(f * slab + band * peers[n], band)],
            ext.at[pl.ds(f * deep + (MARGIN + me) * band, band)],
            bs.at[f, n],
            br.at[f, n],
            "lat",
            peers[n],
        )

    def level_copy(f, way, n):
        level = peers[n] if n < len(peers) else me
        target = ((0, MARGIN + levels)[way] + level) * band
        peer = (jnp.minimum(lev + 1, levs - 1), jnp.maximum(lev - 1, 0))[way]
        if n < len(peers):
            source = ext.at[pl.ds(f * deep + (MARGIN + level) * band, band)]
        else:
            source = ret.at[pl.ds(f * slab + level * band, band)]
        return remote(
            source,
            ext.at[pl.ds(f * deep + target, band)],
            zs.at[f, way, n],
            zr.at[f, way, n],
            "lev",
            peer,
        )

    def level_start(f, n):
        @pl.when(lev < levs - 1)
        def _():
            level_copy(f, 0, n).start()

        @pl.when(lev > 0)
        def _():
            level_copy(f, 1, n).start()

    def spread_remap(step):
        for c in range(2):
            if step or c:

                @pl.when(near(step))
                def _():
                    remap_copy(step, c).start()

    def remap_copy(step, c):
        n = chips - 1 + step
        to = jnp.clip(2 * (chip + step) + (c + core) % 2, 0, levs - 1)
        return remote(rpack.at[to], rrecv.at[lev], rs.at[n, c], rr.at[n, c], "lev", to)

    def remap_arrival(step, c):
        n = chips - 1 + step
        return remote(
            rpack.at[lev], rrecv.at[lev], rs.at[n, c], rr.at[n, c], "lev", lev + 1 - 2 * core
        )

    def relay(way, hop):
        step = (1, -1)[way]

        @pl.when(jnp.logical_and(near(step), near(-step * hop)))
        def _():
            pl.semaphore_signal(
                far.at[way, hop],
                inc=1,
                device_id={"lev": jnp.clip(lev + 2 * step, 0, levs - 1)},
                device_id_type=MESH,
            )

    def pair_copy():
        return remote(hsum, psum, ps, pr, "lev", lev + 1 - 2 * core)

    def sum_copy(d):
        return remote(csum, sums.at[d], ss.at[d], sr.at[d], "lev", jnp.maximum(lev - 2 * d, core))

    def sends(d):
        return lev >= 2 * d if d == chips - 1 else jnp.logical_and(core == 0, lev >= 2 * d)

    def total_copy():
        return remote(below_all, below_all, ts, tr, "lev", lev + 1 - 2 * core)

    ways = range(len(peers))
    for way in range(2):
        relay(way, 1)
    for n in ways:
        for c in coefficient_copy(n):
            c.start()
    for f in range(count):
        for n in ways:
            field_copy(f, n).start()

    for c in loads[3:]:
        c.wait()
    for p in range(levs):
        for r in range(rows):
            lo = p * levels
            ks = lo + lax.broadcasted_iota(jnp.int32, (levels, piece), 0)
            rpack[p, 0, r] = (remap_level[r, lo : lo + levels, :] - ks).astype(jnp.float32)
            rpack[p, 1, r] = remap_weight[r, lo : lo + levels, :]
    for r in range(rows):
        spread(thick, r * cols, band, thickness, (r,))
    spread(surf, 0, cols, surface, ())
    blank = jnp.zeros((SUB, LANES), jnp.float32)
    for f in range(count):
        copy_rows(work, f * room + LOW + band * me, pack, (me * count + f) * band, band)
        for at in (*range(0, LOW, SUB), *(LOW + slab + n for n in range(0, 2 * cols, SUB))):
            work[pl.ds(f * room + at, SUB), :] = blank
    for g in range(4):
        copy_rows(work_c, g * slab + band * me, pack_c, (me * 4 + g) * band, band)
    for at in (*range(0, LOW, SUB), *(LOW + slab + n for n in range(0, 2 * cols, SUB))):
        mid[pl.ds(at, SUB), :] = blank
    for at in range(0, LOW, SUB):
        norths[pl.ds(at, SUB), :] = blank
        easts[pl.ds(at, SUB), :] = blank
    for at in range(0, SUB, SUB):
        easts[pl.ds(LOW + slab + at, SUB), :] = blank
    rrecv[lev] = rpack[lev]
    for step in (-1, 0, 1):
        spread_remap(step)
    for hop in range(1, chips - 1):
        for way in range(2):
            back = -(hop + 1) if way == 0 else hop + 1

            @pl.when(near(back))
            def _():
                pl.semaphore_wait(far.at[way, hop], 1)

            if hop + 1 < chips - 1:
                relay(way, hop + 1)
            spread_remap(back)

    row = lax.broadcasted_iota(jnp.int32, (SUB, LANES), 0)
    lane = lax.broadcasted_iota(jnp.int32, (SUB, LANES), 1)
    last, first, two = lane == LANES - 1, lane < 1, lane < 2

    def substep(source, base, target, to):
        def q(at):
            return source[pl.ds(base + at, SUB), :]

        for p in starts(slab):
            here = q(p)
            o0, o1, c0, c1 = (
                work_c[pl.ds(g * slab + p, SUB), :] for g in (2, 3, 0, 1)
            )
            up = jnp.where(
                o0 < 0.5,
                jnp.where(o0 == 0.0, here, q(p - cols)),
                jnp.where(o0 == 1.0, q(p + cols), q(p + 2 * cols)),
            )
            norths[pl.ds(LOW + p, SUB), :] = c0 * up
            after, before = q(p + 1), q(p - 1)
            end, start = (cols - 1 - p) % cols, -p % cols
            if end < SUB:
                after = jnp.where(row == end, q(p + 1 - cols), after)
            if start < SUB:
                before = jnp.where(row == start, q(p - 1 + cols), before)
            side = jnp.where(
                o1 < 0.5,
                jnp.where(o1 == 0.0, here, pltpu.roll(jnp.where(last, before, here), 1, 1)),
                jnp.where(
                    o1 == 1.0,
                    pltpu.roll(jnp.where(first, after, here), LANES - 1, 1),
                    pltpu.roll(jnp.where(two, after, here), LANES - 2, 1),
                ),
            )
            easts[pl.ds(LOW + p, SUB), :] = c1 * side
        for p in starts(slab):
            north, south = norths[pl.ds(LOW + p, SUB), :], norths[pl.ds(LOW + p - cols, SUB), :]
            east, before = easts[pl.ds(LOW + p, SUB), :], easts[pl.ds(LOW + p - 1, SUB), :]
            start = -p % cols
            if start < SUB:
                before = jnp.where(row == start, easts[pl.ds(LOW + p - 1 + cols, SUB), :], before)
            west = pltpu.roll(jnp.where(last, before, east), 1, 1)
            target[pl.ds(to + p, SUB), :] = q(p) - (north - south) - (east - west)

    for n in ways:
        for c in coefficient_copy(n):
            c.wait_recv()

    def advect(f, carry):
        for n in ways:
            field_copy(f, n).wait_recv()
        substep(work, f * room + LOW, mid, LOW)
        substep(mid, LOW, ret, f * slab)
        for n in ways:
            back_copy(f, n).start()
        level_start(f, len(peers))
        copy_rows(ext, f * deep + (MARGIN + me) * band, ret, f * slab + band * me, band)
        return carry

    lax.fori_loop(0, count, advect, 0)

    for n in ways:
        for c in coefficient_copy(n):
            c.wait_send()
        for f in range(count):
            field_copy(f, n).wait_send()
    for step in range(1 - chips, chips):
        for c in range(2):
            if step or c:

                @pl.when(near(-step))
                def _():
                    remap_arrival(step, c).wait_recv()

                @pl.when(near(step))
                def _():
                    remap_copy(step, c).wait_send()

    for p in range(levs):
        rall[:, :, :, p * piece : (p + 1) * piece] = rrecv[p]
    for g, target in enumerate((delta, weight)):
        for r in range(rows):
            spread(target, r * cols, band, rall, (g, r))

    def heat(k, s):
        at = ext[pl.ds((MARGIN + k) * band + s, SUB), :]
        return at * thick[pl.ds(k * band + s, SUB), :]

    def share(f, carry):
        for n in reversed(ways):
            back_copy(f, n).wait_recv()
            level_start(f, n)
        return carry

    def sent(f, carry):
        for n in ways:
            back_copy(f, n).wait_send()
        return carry

    share(0, 0)
    for s in starts(band):
        hsum[pl.ds(s, SUB), :] = functools.reduce(add_terms, [heat(k, s) for k in range(levels)])
    pair_copy().start()
    pair_copy().wait_recv()
    for s in starts(band):
        csum[pl.ds(s, SUB), :] = hsum[pl.ds(s, SUB), :] + psum[pl.ds(s, SUB), :]
    for d in range(1, levs // 2):

        @pl.when(sends(d))
        def _():
            sum_copy(d).start()

    lax.fori_loop(1, count, share, 0)
    lax.fori_loop(0, count, sent, 0)

    def remap(f, carry):
        base = f * deep

        @pl.when(lev > 0)
        def _():
            for n in range(lats):
                level_copy(f, 0, n).wait_recv()
                level_copy(f, 1, n).wait_send()

        @pl.when(lev < levs - 1)
        def _():
            for n in range(lats):
                level_copy(f, 1, n).wait_recv()
                level_copy(f, 0, n).wait_send()

        @pl.when(lev == 0)
        def _():
            for m in range(MARGIN):
                copy_rows(ext, base + m * band, ext, base + MARGIN * band, band)

        @pl.when(lev == levs - 1)
        def _():
            end = base + (MARGIN + levels) * band
            for m in range(MARGIN):
                copy_rows(ext, end + m * band, ext, end - band, band)

        for s in starts(band):
            q = [ext[pl.ds(base + m * band + s, SUB), :] for m in range(levels + 2 * MARGIN)]
            edge = {
                m: (7.0 * (q[m - 1] + q[m]) - (q[m - 2] + q[m + 1])) * (1.0 / 12.0)
                for m in range(2, levels + 2 * MARGIN - 1)
            }
            for k in range(levels):
                dk = delta[pl.ds(k * band + s, SUB), :]
                wk = weight[pl.ds(k * band + s, SUB), :]
                at = k + MARGIN
                centre, left, right = q[at - 2], edge[at - 2], edge[at - 1]
                for o in range(-1, 3):
                    chosen = dk == float(o)
                    centre = jnp.where(chosen, q[at + o], centre)
                    left = jnp.where(chosen, edge[at + o], left)
                    right = jnp.where(chosen, edge[at + o + 1], right)
                curve = 6.0 * centre - 3.0 * (left + right)
                value[pl.ds(k * band + s, SUB), :] = left + wk * (
                    (right - left) + curve * (1.0 - wk)
                )
        for r in range(rows):
            for c in range(cols):
                out[f, r, :, c * LANES : (c + 1) * LANES] = value[
                    pl.ds(r * cols + c, levels, stride=band), :
                ]
        return carry

    lax.fori_loop(0, count - 1, remap, 0)
    @pl.when(core == 0)
    def _():
        for d in range(1, chips - 1):

            @pl.when(chip + d < chips)
            def _():
                sum_copy(d).wait_recv()

        for s in starts(band):
            total = jnp.zeros((SUB, LANES), jnp.float32)
            for d in range(1, chips - 1):
                more = sums[d, pl.ds(s, SUB), :]
                total = total + jnp.where(chip + d < chips, more, jnp.zeros_like(more))
            below_all[pl.ds(s, SUB), :] = total
        total_copy().start()

    remap(count - 1, 0)

    @pl.when(core == 1)
    def _():
        total_copy().wait_recv()

    @pl.when(chip == 0)
    def _():
        sum_copy(chips - 1).wait_recv()

    for s in starts(band):
        pair, far_sum = psum[pl.ds(s, SUB), :], sums[chips - 1, pl.ds(s, SUB), :]
        below = surf[pl.ds(s, SUB), :] + below_all[pl.ds(s, SUB), :]
        below = below + jnp.where(chip == 0, far_sum, jnp.zeros_like(pair))
        below = below + jnp.where(core == 0, pair, jnp.zeros_like(pair))
        for k in range(levels - 1, -1, -1):
            term = heat(k, s)
            value[pl.ds(k * band + s, SUB), :] = below + 0.5 * term
            below = below + term
    for r in range(rows):
        for c in range(cols):
            geo[r, :, c * LANES : (c + 1) * LANES] = value[
                pl.ds(r * cols + c, levels, stride=band), :
            ]

    pair_copy().wait_send()

    @pl.when(core == 0)
    def _():
        total_copy().wait_send()

    for d in range(1, chips):

        @pl.when(sends(d))
        def _():
            sum_copy(d).wait_send()


def fused(lats, levs, *args):
    state, courant, offsets, thickness, surface, level, weight = args
    count, rows, levels, width = state.shape
    piece = level.shape[2]
    cols = width // LANES
    band = rows * cols
    slab = band * lats
    room = LOW + slab + -(-2 * cols // SUB) * SUB
    room = -(-room // SUB) * SUB
    f32 = jnp.float32
    dma = pltpu.SemaphoreType.DMA

    def tall(n):
        return pltpu.VMEM((-(-n // SUB) * SUB, LANES), f32)

    return pl.pallas_call(
        functools.partial(kernel, lats, levs),
        out_shape=(pltpu.VMEM(state.shape, f32), pltpu.VMEM(thickness.shape, f32)),
        in_specs=[pl.BlockSpec(memory_space=pl.ANY)] * 7,
        scratch_shapes=[
            *(pltpu.VMEM(x.shape, x.dtype) for x in args),
            tall(levels * count * band),
            tall(levels * 4 * band),
            tall(4 * slab),
            tall(count * room),
            tall(room),
            tall(LOW + slab),
            tall(LOW + slab + SUB),
            tall(count * slab),
            tall(count * (levels + 2 * MARGIN) * band),
            pltpu.VMEM((levs, 2, rows, levels, piece), f32),
            pltpu.VMEM((levs, 2, rows, levels, piece), f32),
            pltpu.VMEM((2, rows, levels, width), f32),
            tall(levels * band),
            tall(levels * band),
            tall(levels * band),
            tall(band),
            tall(band),
            tall(band),
            tall(band),
            pltpu.VMEM((levs // 2, -(-band // SUB) * SUB, LANES), f32),
            tall(band),
            tall(levels * band),
            dma((7,)),
            dma((count + 4, lats)),
            dma((count + 4, lats)),
            dma((count, lats)),
            dma((count, lats)),
            dma((count, 2, lats)),
            dma((count, 2, lats)),
            dma((levs, 2)),
            dma((levs, 2)),
            dma,
            dma,
            dma((levs // 2,)),
            dma((levs // 2,)),
            dma,
            dma,
            pltpu.SemaphoreType.REGULAR((2, levs // 2)),
        ],
        compiler_params=pltpu.CompilerParams(collective_id=0, has_side_effects=True),
    )(*args)


def solution(mesh):
    in_specs = (
        P(None, "lat", "lev", None),
        P(None, "lat", "lev", None),
        P(None, "lat", "lev", None),
        P("lat", "lev", None),
        P("lat", None),
        P("lat", None, "lev"),
        P("lat", None, "lev"),
    )
    out_specs = (P(None, "lat", "lev", None), P("lat", "lev", None))
    lats, levs = mesh.shape["lat"], mesh.shape["lev"]

    def body(state, *rest):
        count, rows, levels, width = state.shape
        small = width % LANES or rows * (width // LANES) < SUB or LOW < width // LANES
        if levels != lats or levels != MARGIN or small or levs % 2 or levs < 4 or count < 2:
            return per_device(state, *rest)
        return fused(lats, levs, state, *rest)

    return jax.shard_map(
        body, mesh=mesh, in_specs=in_specs, out_specs=out_specs, check_vma=False
    )
```

```python
import functools

import jax
import jax.numpy as jnp
from jax import lax
from jax.experimental import pallas as pl
from jax.experimental.pallas import tpu as pltpu
from jax.sharding import PartitionSpec as P

SUBSTEPS = 2


def extended_2(block, sides, width):
    for axis, dim in sides:
        count = lax.axis_size(axis)
        forward = [(i, i + 1) for i in range(count - 1)]
        backward = [(target, source) for source, target in forward]
        low = lax.ppermute(
            lax.slice_in_dim(block, block.shape[dim] - width, None, axis=dim), axis, forward
        )
        high = lax.ppermute(lax.slice_in_dim(block, 0, width, axis=dim), axis, backward)
        block = jnp.concatenate([low, block, high], axis=dim)
    return block


def from_behind(x, axis, by):
    count = lax.axis_size(axis)
    pairs = [(i, i + by) for i in range(count) if 0 <= i + by < count]
    return lax.ppermute(x, axis, pairs)


def entering(x, axis, combine, identity):
    count, position = (lax.axis_size(axis), lax.axis_index(axis))
    everything = lax.all_gather(x, axis)
    start = jnp.broadcast_to(jnp.asarray(identity, x.dtype), x.shape)

    def lap(k, before):
        at = count - 1 - k
        reached = at > position
        new = combine(before, everything[at])
        return jnp.where(reached, new, before)

    return lax.fori_loop(0, count, lap, start)


def local_parabola(extended, delta, weight):
    margin = 4
    count = extended.shape[-2] - 2 * margin
    edges = (
        7.0 * (extended[..., 1:-2, :] + extended[..., 2:-1, :])
        - (extended[..., :-3, :] + extended[..., 3:, :])
    ) / 12.0
    centre = jnp.zeros(extended.shape[:-2] + (count, extended.shape[-1]), jnp.float32)
    left = centre
    right = centre
    for offset in range(-2, 3):
        chosen = delta == offset
        start = margin + offset
        centre = jnp.where(chosen, extended[..., start : start + count, :], centre)
        left = jnp.where(chosen, edges[..., start - 2 : start - 2 + count, :], left)
        right = jnp.where(chosen, edges[..., start - 1 : start - 1 + count, :], right)
    slope = right - left
    curve = 6.0 * centre - 3.0 * (left + right)
    return left + weight * (slope + curve * (1.0 - weight))


def add_terms(earlier, later):
    return earlier + later


def per_device(state, courant, offsets, log_thickness, surface, remap_level, remap_weight):
    count, rows, levels, width = state.shape
    north_masks = [offsets[0] == offset for offset in range(-1, 3)]
    east_masks = [offsets[1] == offset for offset in range(-1, 3)]
    field = state
    for substep in range(SUBSTEPS):
        padded = extended_2(field, (("lat", 1),), 2)
        picked = jnp.zeros_like(field)
        for number, offset in enumerate(range(-1, 3)):
            picked = jnp.where(
                north_masks[number][None], padded[:, offset + 2 : offset + 2 + rows], picked
            )
        north = courant[0][None] * picked
        below = from_behind(north[:, rows - 1 :], "lat", 1)
        south = jnp.concatenate([below, north[:, : rows - 1]], axis=1)
        moved = jnp.zeros_like(field)
        for number, offset in enumerate(range(-1, 3)):
            moved = jnp.where(east_masks[number][None], jnp.roll(field, -offset, axis=3), moved)
        east = courant[1][None] * moved
        west = jnp.roll(east, 1, axis=3)
        field = field - (north - south) - (east - west)
    heating = field[0] * log_thickness
    lower = [jnp.zeros_like(heating[:, 0])]
    for level in range(levels - 1, 0, -1):
        lower.insert(0, lower[0] + heating[:, level])
    lower_local = jnp.stack(lower, axis=1)
    column_sum = jnp.sum(heating, axis=1)
    deeper = entering(column_sum, "lev", add_terms, jnp.zeros_like(column_sum))
    geopotential = surface[:, None, :] + deeper[:, None, :] + lower_local + 0.5 * heating
    total_levels = remap_level.shape[1]
    delta_col = (remap_level - jnp.arange(total_levels, dtype=jnp.int32)[None, :, None]).astype(
        jnp.float32
    )
    inputs = lax.all_to_all(
        jnp.stack([delta_col, remap_weight]), "lev", split_axis=2, concat_axis=3, tiled=True
    )
    margin = 4
    lev = lax.axis_index("lev")
    before = from_behind(field, "lev", 1)[:, :, levels - margin :]
    after = from_behind(field, "lev", -1)[:, :, :margin]
    before = jnp.where(lev == 0, field[:, :, :1], before)
    after = jnp.where(lev == lax.axis_size("lev") - 1, field[:, :, levels - 1 :], after)
    extended = jnp.concatenate([before, field, after], axis=2)
    remapped = local_parabola(extended, inputs[0][None], inputs[1][None])
    return (remapped, geopotential)


MARGIN = 4
DIRECT = 2
LANES = 128
SUB = 8
MESH = pl.DeviceIdType.MESH


def remote(src, dst, send, recv, axis, peer, other=None):
    return pltpu.make_async_remote_copy(
        src_ref=src,
        dst_ref=dst,
        send_sem=send,
        recv_sem=recv,
        device_id={axis: peer, **(other or {})},
        device_id_type=MESH,
    )


def starts(count):
    return [min(at, count - SUB) for at in range(0, count, SUB)]


def copy_rows(target, to, source, at, count):
    for s in starts(count):
        target[pl.ds(to + s, SUB), :] = source[pl.ds(at + s, SUB), :]


def kernel(lats, levs, *refs):
    (
        h_state,
        h_courant,
        h_offsets,
        h_thickness,
        h_surface,
        h_level,
        h_weight,
        out,
        geo,
        state,
        courant,
        offsets,
        thickness,
        surface,
        remap_level,
        remap_weight,
        pack,
        pack_c,
        work_c,
        work,
        mid,
        taps,
        ret,
        ext,
        rpack,
        rrecv,
        rall,
        delta,
        weight,
        thick,
        surf,
        hsum,
        psum,
        csum,
        sums,
        value,
        ins,
        fs,
        fr,
        bs,
        br,
        zs,
        zr,
        rs,
        rr,
        ps,
        pr,
        ss,
        sr,
        far,
        side,
    ) = refs
    count, rows, levels, width = state.shape
    cols = width // LANES
    band = rows * cols
    slab = band * lats
    room = work.shape[0] // count
    low = -(-2 * cols // SUB) * SUB
    deep = (levels + 2 * MARGIN) * band
    piece = remap_level.shape[2]
    early = count - min(DIRECT, count - 1)
    me = lax.axis_index("lat")
    lev = lax.axis_index("lev")
    core = lax.rem(lev, 2)
    if lats == 4:
        across = lax.rem(me + 2, lats)
        peers = [lats - 1 - me, across, lats - 1 - across]
    else:
        peers = [lax.rem(me + d, lats) for d in range(1, lats)]

    barrier = pltpu.get_barrier_semaphore()
    chips = levs // 2
    chip = lev // 2
    for peer in peers:
        pl.semaphore_signal(barrier, inc=1, device_id={"lat": peer}, device_id_type=MESH)
    pl.semaphore_signal(
        barrier, inc=1, device_id={"lev": lev + 1 - 2 * core}, device_id_type=MESH
    )

    def near(step):
        return jnp.logical_and(chip + step >= 0, chip + step < chips)

    for step in (-1, 1):
        for c in range(2):

            @pl.when(near(step))
            def _():
                pl.semaphore_signal(
                    barrier,
                    inc=1,
                    device_id={"lev": jnp.clip(2 * (chip + step) + c, 0, levs - 1)},
                    device_id_type=MESH,
                )

    loads = [
        pltpu.make_async_copy(a, b, ins.at[n])
        for n, (a, b) in enumerate(
            (
                (h_courant, courant),
                (h_offsets, offsets),
                (h_state, state),
                (h_level, remap_level),
                (h_weight, remap_weight),
                (h_thickness, thickness),
                (h_surface, surface),
            )
        )
    ]
    for c in loads:
        c.start()

    def spread(target, first, stride, tile, where):
        for c in range(cols):
            target[pl.ds(first + c, tile.shape[-2], stride=stride), :] = tile[
                (*where, slice(None), slice(c * LANES, (c + 1) * LANES))
            ]

    for c in loads[:3]:
        c.wait()
    for r in range(rows):
        for g in range(2):
            for c in range(cols):
                lanes = slice(c * LANES, (c + 1) * LANES)
                pack_c[pl.ds(g * band + r * cols + c, levels, stride=4 * band), :] = courant[
                    g, r, :, lanes
                ]
                pack_c[pl.ds((g + 2) * band + r * cols + c, levels, stride=4 * band), :] = offsets[
                    g, r, :, lanes
                ].astype(jnp.float32)
    for f in range(count):
        for r in range(rows):
            spread(pack, f * band + r * cols, count * band, state, (f, r))

    sides = (chip > 0).astype(jnp.int32) + (chip < chips - 1).astype(jnp.int32)
    pl.semaphore_wait(barrier, len(peers) + 1 + 2 * sides)

    def coefficient_copy(n):
        return [
            remote(
                pack_c.at[pl.ds((peers[n] * 4 + g) * band, band)],
                work_c.at[pl.ds(g * room + low + band * me, band)],
                fs.at[count + g, n],
                fr.at[count + g, n],
                "lat",
                peers[n],
            )
            for g in range(4)
        ]

    def field_copy(f, n):
        return remote(
            pack.at[pl.ds((peers[n] * count + f) * band, band)],
            work.at[pl.ds(f * room + low + band * me, band)],
            fs.at[f, n],
            fr.at[f, n],
            "lat",
            peers[n],
        )

    def back_copy(f, n):
        return remote(
            ret.at[pl.ds(f * slab + band * peers[n], band)],
            ext.at[pl.ds(f * deep + (MARGIN + me) * band, band)],
            bs.at[f, n],
            br.at[f, n],
            "lat",
            peers[n],
        )

    def level_copy(f, way, n):
        level = peers[n] if n < len(peers) else me
        target = ((0, MARGIN + levels)[way] + level) * band
        peer = (jnp.minimum(lev + 1, levs - 1), jnp.maximum(lev - 1, 0))[way]
        if n < len(peers):
            source = ext.at[pl.ds(f * deep + (MARGIN + level) * band, band)]
        else:
            source = ret.at[pl.ds(f * slab + level * band, band)]
        return remote(
            source,
            ext.at[pl.ds(f * deep + target, band)],
            zs.at[f, way, n],
            zr.at[f, way, n],
            "lev",
            peer,
        )

    def direct_copy(f, way, n):
        target = ((0, MARGIN + levels)[way] + me) * band
        peer = (jnp.minimum(lev + 1, levs - 1), jnp.maximum(lev - 1, 0))[way]
        return remote(
            ret.at[pl.ds(f * slab + band * peers[n], band)],
            ext.at[pl.ds(f * deep + target, band)],
            zs.at[f, way, n],
            zr.at[f, way, n],
            "lev",
            peer,
            {"lat": peers[n]},
        )

    up = jnp.logical_and(core == 1, lev < levs - 1)
    down = jnp.logical_and(core == 0, lev > 0)

    def direct_start(f):
        @pl.when(up)
        def _():
            for n in ways:
                direct_copy(f, 0, n).start()

        @pl.when(down)
        def _():
            for n in ways:
                direct_copy(f, 1, n).start()

    def inside_start(f, n):
        @pl.when(core == 0)
        def _():
            level_copy(f, 0, n).start()

        @pl.when(core == 1)
        def _():
            level_copy(f, 1, n).start()

    def level_start(f, n):
        @pl.when(lev < levs - 1)
        def _():
            level_copy(f, 0, n).start()

        @pl.when(lev > 0)
        def _():
            level_copy(f, 1, n).start()

    def spread_remap(step):
        for c in range(2):
            if step or c:

                @pl.when(near(step))
                def _():
                    remap_copy(step, c).start()

    def remap_copy(step, c):
        n = chips - 1 + step
        to = jnp.clip(2 * (chip + step) + (c + core) % 2, 0, levs - 1)
        return remote(rpack.at[to], rrecv.at[lev], rs.at[n, c], rr.at[n, c], "lev", to)

    def remap_arrival(step, c):
        n = chips - 1 + step
        return remote(
            rpack.at[lev], rrecv.at[lev], rs.at[n, c], rr.at[n, c], "lev", lev + 1 - 2 * core
        )

    def relay(way, hop):
        step = (1, -1)[way]

        @pl.when(jnp.logical_and(near(step), near(-step * hop)))
        def _():
            pl.semaphore_signal(
                far.at[way, hop],
                inc=1,
                device_id={"lev": jnp.clip(lev + 2 * step, 0, levs - 1)},
                device_id_type=MESH,
            )

    def pair_copy():
        return remote(hsum, psum, ps, pr, "lev", lev + 1 - 2 * core)

    def sum_copy(d):
        return remote(csum, sums.at[d], ss.at[d], sr.at[d], "lev", jnp.maximum(lev - 2 * d, core))

    def far_copy(c):
        at, to = chips - 1, jnp.maximum(2 * (chip - chips + 1), 0) + (c + core) % 2
        return remote(hsum, sums.at[at + core], ss.at[at + c], sr.at[at + core], "lev", to)

    def far_arrival(c):
        at = chips - 1 + c
        return remote(hsum, sums.at[at], ss.at[at], sr.at[at], "lev", lev + 1 - 2 * core)

    ways = range(len(peers))
    for way in range(2):
        relay(way, 1)
    for n in ways:
        pl.semaphore_signal(
            side.at[n], inc=1, device_id={"lat": peers[n]}, device_id_type=MESH
        )
    for n in ways:
        for c in coefficient_copy(n):
            c.start()
    for f in range(count):
        for n in ways:
            field_copy(f, n).start()

    for c in loads[3:]:
        c.wait()
    for p in range(levs):
        for r in range(rows):
            lo = p * levels
            ks = lo + lax.broadcasted_iota(jnp.int32, (levels, piece), 0)
            rpack[p, 0, r] = (remap_level[r, lo : lo + levels, :] - ks).astype(jnp.float32)
            rpack[p, 1, r] = remap_weight[r, lo : lo + levels, :]
    for r in range(rows):
        spread(thick, r * cols, band, thickness, (r,))
    spread(surf, 0, cols, surface, ())
    blank = jnp.zeros((SUB, LANES), jnp.float32)
    edges = [min(at, room - SUB) for at in (*range(0, low, SUB), *range(low + slab, room, SUB))]
    for f in range(count):
        copy_rows(work, f * room + low + band * me, pack, (me * count + f) * band, band)
        for at in edges:
            work[pl.ds(f * room + at, SUB), :] = blank
    for at in edges:
        mid[pl.ds(at, SUB), :] = blank
        for g in range(4):
            work_c[pl.ds(g * room + at, SUB), :] = blank
    for g in range(4):
        copy_rows(work_c, g * room + low + band * me, pack_c, (me * 4 + g) * band, band)
    rrecv[lev] = rpack[lev]
    for step in (-1, 0, 1):
        spread_remap(step)
    for hop in range(1, chips - 1):
        for way in range(2):
            back = -(hop + 1) if way == 0 else hop + 1

            @pl.when(near(back))
            def _():
                pl.semaphore_wait(far.at[way, hop], 1)

            if hop + 1 < chips - 1:
                relay(way, hop + 1)
            spread_remap(back)

    row = lax.broadcasted_iota(jnp.int32, (SUB, LANES), 0)
    lane = lax.broadcasted_iota(jnp.int32, (SUB, LANES), 1)
    masks = {1: lane == LANES - 1, 2: lane >= LANES - 2, -1: lane < 1, -2: lane < 2}

    def beside(source, base, p, here, shifts):
        found = []
        for way in (1, -1):
            some = [s for s in shifts if s * way > 0]
            if not some:
                continue
            near_by = source[pl.ds(base + p - way, SUB), :]
            at = (-p if way == 1 else cols - 1 - p) % cols
            if at < SUB:
                wrapped = source[pl.ds(base + p - way + way * cols, SUB), :]
                near_by = jnp.where(row == at, wrapped, near_by)
            for s in some:
                mixed = jnp.where(masks[s], near_by, here)
                found.append(pltpu.roll(mixed, s % LANES, 1))
        return found

    def substep(source, base, target, to):
        for p in starts(slab):
            here = source[pl.ds(base + p, SUB), :]
            terms = [here, *beside(source, base, p, here, (1, 2, -1, -2))]
            terms += [source[pl.ds(base + p + d * cols, SUB), :] for d in (-1, -2, 1, 2)]
            products = [taps[pl.ds(g * slab + p, SUB), :] * q for g, q in enumerate(terms)]
            while len(products) > 1:
                pairs = [x + y for x, y in zip(products[::2], products[1::2])]
                products = pairs + products[2 * len(pairs) :]
            target[pl.ds(to + p, SUB), :] = products[0]

    for n in ways:
        for c in coefficient_copy(n):
            c.wait_recv()
    none = jnp.zeros((SUB, LANES), jnp.float32)
    for p in starts(slab):
        c0, c1, o0, o1 = (work_c[pl.ds(g * room + low + p, SUB), :] for g in range(4))
        under, under_o = (work_c[pl.ds(g * room + low + p - cols, SUB), :] for g in (0, 2))
        back, back_o = (
            beside(work_c, g * room + low, p, here, (1,))[0] for g, here in ((1, c1), (3, o1))
        )
        middle = none + 1.0
        for first, near_c, near_o, far_c, far_o in ((1, c1, o1, back, back_o), (5, c0, o0, under, under_o)):
            own = [jnp.where(near_o == float(o), near_c, none) for o in range(-1, 3)]
            other = [jnp.where(far_o == float(o), far_c, none) for o in range(-1, 3)]
            middle = middle + (other[2] - own[1])
            for g, tap in enumerate((other[1] - own[0], other[0], other[3] - own[2], -own[3])):
                taps[pl.ds((first + g) * slab + p, SUB), :] = tap
        taps[pl.ds(p, SUB), :] = middle

    def advect(f, direct):
        for n in ways:
            field_copy(f, n).wait_recv()
        substep(work, f * room + low, mid, low)
        substep(mid, low, ret, f * slab)
        if direct:
            direct_start(f)
        for n in ways:
            back_copy(f, n).start()
        level_start(f, len(peers))
        copy_rows(ext, f * deep + (MARGIN + me) * band, ret, f * slab + band * me, band)

    def loop(first, end, body, *rest):
        def step(f, carry):
            body(f, *rest)
            return carry

        lax.fori_loop(first, end, step, 0)

    loop(0, early, advect, False)
    for n in ways:
        pl.semaphore_wait(side.at[n], 1)
    loop(early, count, advect, True)

    for n in ways:
        for c in coefficient_copy(n):
            c.wait_send()
        for f in range(count):
            field_copy(f, n).wait_send()
    for step in range(1 - chips, chips):
        for c in range(2):
            if step or c:

                @pl.when(near(-step))
                def _():
                    remap_arrival(step, c).wait_recv()

                @pl.when(near(step))
                def _():
                    remap_copy(step, c).wait_send()

    for p in range(levs):
        rall[:, :, :, p * piece : (p + 1) * piece] = rrecv[p]
    for g, target in enumerate((delta, weight)):
        for r in range(rows):
            spread(target, r * cols, band, rall, (g, r))

    def heat(k, s):
        at = ext[pl.ds((MARGIN + k) * band + s, SUB), :]
        return at * thick[pl.ds(k * band + s, SUB), :]

    def share(f, direct):
        for n in reversed(ways):
            back_copy(f, n).wait_recv()
            (inside_start if direct else level_start)(f, n)

    def sent(f):
        for n in ways:
            back_copy(f, n).wait_send()

    for n in ways:
        back_copy(0, n).wait_recv()
    for s in starts(band):
        hsum[pl.ds(s, SUB), :] = functools.reduce(add_terms, [heat(k, s) for k in range(levels)])

    @pl.when(chip == chips - 1)
    def _():
        for c in range(2):
            far_copy(c).start()

    pair_copy().start()
    for n in ways:
        level_start(0, n)
    pair_copy().wait_recv()
    for s in starts(band):
        csum[pl.ds(s, SUB), :] = hsum[pl.ds(s, SUB), :] + psum[pl.ds(s, SUB), :]
    for d in range(1, chips - 1):

        @pl.when(chip >= d)
        def _():
            sum_copy(d).start()

    loop(1, early, share, False)
    loop(early, count, share, True)
    loop(0, count, sent)

    def remap(f):
        base = f * deep

        @pl.when(lev > 0)
        def _():
            for n in range(lats):
                level_copy(f, 0, n).wait_recv()
                level_copy(f, 1, n).wait_send()

        @pl.when(lev < levs - 1)
        def _():
            for n in range(lats):
                level_copy(f, 1, n).wait_recv()
                level_copy(f, 0, n).wait_send()

        @pl.when(lev == 0)
        def _():
            for m in range(MARGIN):
                copy_rows(ext, base + m * band, ext, base + MARGIN * band, band)

        @pl.when(lev == levs - 1)
        def _():
            end = base + (MARGIN + levels) * band
            for m in range(MARGIN):
                copy_rows(ext, end + m * band, ext, end - band, band)

        for s in starts(band):
            q = [ext[pl.ds(base + m * band + s, SUB), :] for m in range(levels + 2 * MARGIN)]
            edge = {
                m: (7.0 * (q[m - 1] + q[m]) - (q[m - 2] + q[m + 1])) * (1.0 / 12.0)
                for m in range(2, levels + 2 * MARGIN - 1)
            }
            for k in range(levels):
                dk = delta[pl.ds(k * band + s, SUB), :]
                wk = weight[pl.ds(k * band + s, SUB), :]
                at = k + MARGIN
                centre, left, right = q[at - 2], edge[at - 2], edge[at - 1]
                for o in range(-1, 3):
                    chosen = dk == float(o)
                    centre = jnp.where(chosen, q[at + o], centre)
                    left = jnp.where(chosen, edge[at + o], left)
                    right = jnp.where(chosen, edge[at + o + 1], right)
                curve = 6.0 * centre - 3.0 * (left + right)
                value[pl.ds(k * band + s, SUB), :] = left + wk * (
                    (right - left) + curve * (1.0 - wk)
                )
        for r in range(rows):
            for c in range(cols):
                out[f, r, :, c * LANES : (c + 1) * LANES] = value[
                    pl.ds(r * cols + c, levels, stride=band), :
                ]

    loop(0, count, remap)
    for d in range(1, chips - 1):

        @pl.when(chip + d < chips)
        def _():
            sum_copy(d).wait_recv()

    @pl.when(chip == 0)
    def _():
        for c in range(2):
            far_arrival(c).wait_recv()

    for s in starts(band):
        below = surf[pl.ds(s, SUB), :]
        for here, more in (
            (core == 0, psum[pl.ds(s, SUB), :]),
            *((chip + d < chips, sums[d, pl.ds(s, SUB), :]) for d in range(1, chips - 1)),
            *((chip == 0, sums[chips - 1 + c, pl.ds(s, SUB), :]) for c in range(2)),
        ):
            below = below + jnp.where(here, more, jnp.zeros_like(more))
        for k in range(levels - 1, -1, -1):
            term = heat(k, s)
            value[pl.ds(k * band + s, SUB), :] = below + 0.5 * term
            below = below + term
    for r in range(rows):
        for c in range(cols):
            geo[r, :, c * LANES : (c + 1) * LANES] = value[
                pl.ds(r * cols + c, levels, stride=band), :
            ]

    pair_copy().wait_send()

    @pl.when(chip == chips - 1)
    def _():
        for c in range(2):
            far_copy(c).wait_send()

    for d in range(1, chips - 1):

        @pl.when(chip >= d)
        def _():
            sum_copy(d).wait_send()


def leave(out, geo, h_out, h_geo, sems):
    copies = [
        pltpu.make_async_copy(a, b, sems.at[n])
        for n, (a, b) in enumerate(((out, h_out), (geo, h_geo)))
    ]
    for c in copies:
        c.start()
    for c in copies:
        c.wait()


def fused(lats, levs, *args):
    state, courant, offsets, thickness, surface, level, weight = args
    count, rows, levels, width = state.shape
    piece = level.shape[2]
    cols = width // LANES
    band = rows * cols
    slab = band * lats
    room = -(-(slab + 2 * (-(-2 * cols // SUB) * SUB)) // SUB) * SUB
    f32 = jnp.float32
    dma = pltpu.SemaphoreType.DMA

    def tall(n):
        return pltpu.VMEM((-(-n // SUB) * SUB, LANES), f32)

    results = pl.pallas_call(
        functools.partial(kernel, lats, levs),
        out_shape=(pltpu.VMEM(state.shape, f32), pltpu.VMEM(thickness.shape, f32)),
        in_specs=[pl.BlockSpec(memory_space=pl.ANY)] * 7,
        scratch_shapes=[
            *(pltpu.VMEM(x.shape, x.dtype) for x in args),
            tall(levels * count * band),
            tall(levels * 4 * band),
            tall(4 * room),
            tall(count * room),
            tall(room),
            tall(9 * slab),
            tall(count * slab),
            tall(count * (levels + 2 * MARGIN) * band),
            pltpu.VMEM((levs, 2, rows, levels, piece), f32),
            pltpu.VMEM((levs, 2, rows, levels, piece), f32),
            pltpu.VMEM((2, rows, levels, width), f32),
            tall(levels * band),
            tall(levels * band),
            tall(levels * band),
            tall(band),
            tall(band),
            tall(band),
            tall(band),
            pltpu.VMEM((levs // 2 + 1, -(-band // SUB) * SUB, LANES), f32),
            tall(levels * band),
            dma((7,)),
            dma((count + 4, lats)),
            dma((count + 4, lats)),
            dma((count, lats)),
            dma((count, lats)),
            dma((count, 2, lats)),
            dma((count, 2, lats)),
            dma((levs, 2)),
            dma((levs, 2)),
            dma,
            dma,
            dma((levs // 2 + 1,)),
            dma((levs // 2 + 1,)),
            pltpu.SemaphoreType.REGULAR((2, levs // 2)),
            pltpu.SemaphoreType.REGULAR((lats,)),
        ],
        compiler_params=pltpu.CompilerParams(collective_id=0, has_side_effects=True),
    )(*args)
    results = [pltpu.with_memory_space_constraint(x, pltpu.VMEM) for x in results]
    return pl.pallas_call(
        leave,
        out_shape=tuple(pltpu.HBM(x.shape, x.dtype) for x in results),
        in_specs=[pl.BlockSpec(memory_space=pltpu.VMEM)] * 2,
        out_specs=(pl.BlockSpec(memory_space=pltpu.HBM),) * 2,
        scratch_shapes=[dma((2,))],
    )(*results)


def solution(mesh):
    in_specs = (
        P(None, "lat", "lev", None),
        P(None, "lat", "lev", None),
        P(None, "lat", "lev", None),
        P("lat", "lev", None),
        P("lat", None),
        P("lat", None, "lev"),
        P("lat", None, "lev"),
    )
    out_specs = (P(None, "lat", "lev", None), P("lat", "lev", None))
    lats, levs = mesh.shape["lat"], mesh.shape["lev"]

    def body(state, *rest):
        count, rows, levels, width = state.shape
        small = width % LANES or rows * (width // LANES) < SUB
        if levels != lats or levels != MARGIN or small or levs % 2 or levs < 4 or count < 2:
            return per_device(state, *rest)
        return fused(lats, levs, state, *rest)

    return jax.shard_map(
        body, mesh=mesh, in_specs=in_specs, out_specs=out_specs, check_vma=False
    )
```

```python
import functools

import jax
import jax.numpy as jnp
from jax import lax
from jax.experimental import pallas as pl
from jax.experimental.pallas import tpu as pltpu
from jax.sharding import PartitionSpec as P

SUBSTEPS = 2


def extended_2(block, sides, width):
    for axis, dim in sides:
        count = lax.axis_size(axis)
        forward = [(i, i + 1) for i in range(count - 1)]
        backward = [(target, source) for source, target in forward]
        low = lax.ppermute(
            lax.slice_in_dim(block, block.shape[dim] - width, None, axis=dim), axis, forward
        )
        high = lax.ppermute(lax.slice_in_dim(block, 0, width, axis=dim), axis, backward)
        block = jnp.concatenate([low, block, high], axis=dim)
    return block


def from_behind(x, axis, by):
    count = lax.axis_size(axis)
    pairs = [(i, i + by) for i in range(count) if 0 <= i + by < count]
    return lax.ppermute(x, axis, pairs)


def entering(x, axis, combine, identity):
    count, position = (lax.axis_size(axis), lax.axis_index(axis))
    everything = lax.all_gather(x, axis)
    start = jnp.broadcast_to(jnp.asarray(identity, x.dtype), x.shape)

    def lap(k, before):
        at = count - 1 - k
        reached = at > position
        new = combine(before, everything[at])
        return jnp.where(reached, new, before)

    return lax.fori_loop(0, count, lap, start)


def local_parabola(extended, delta, weight):
    margin = 4
    count = extended.shape[-2] - 2 * margin
    edges = (
        7.0 * (extended[..., 1:-2, :] + extended[..., 2:-1, :])
        - (extended[..., :-3, :] + extended[..., 3:, :])
    ) / 12.0
    centre = jnp.zeros(extended.shape[:-2] + (count, extended.shape[-1]), jnp.float32)
    left = centre
    right = centre
    for offset in range(-2, 3):
        chosen = delta == offset
        start = margin + offset
        centre = jnp.where(chosen, extended[..., start : start + count, :], centre)
        left = jnp.where(chosen, edges[..., start - 2 : start - 2 + count, :], left)
        right = jnp.where(chosen, edges[..., start - 1 : start - 1 + count, :], right)
    slope = right - left
    curve = 6.0 * centre - 3.0 * (left + right)
    return left + weight * (slope + curve * (1.0 - weight))


def add_terms(earlier, later):
    return earlier + later


def per_device(state, courant, offsets, log_thickness, surface, remap_level, remap_weight):
    count, rows, levels, width = state.shape
    north_masks = [offsets[0] == offset for offset in range(-1, 3)]
    east_masks = [offsets[1] == offset for offset in range(-1, 3)]
    field = state
    for substep in range(SUBSTEPS):
        padded = extended_2(field, (("lat", 1),), 2)
        picked = jnp.zeros_like(field)
        for number, offset in enumerate(range(-1, 3)):
            picked = jnp.where(
                north_masks[number][None], padded[:, offset + 2 : offset + 2 + rows], picked
            )
        north = courant[0][None] * picked
        below = from_behind(north[:, rows - 1 :], "lat", 1)
        south = jnp.concatenate([below, north[:, : rows - 1]], axis=1)
        moved = jnp.zeros_like(field)
        for number, offset in enumerate(range(-1, 3)):
            moved = jnp.where(east_masks[number][None], jnp.roll(field, -offset, axis=3), moved)
        east = courant[1][None] * moved
        west = jnp.roll(east, 1, axis=3)
        field = field - (north - south) - (east - west)
    heating = field[0] * log_thickness
    lower = [jnp.zeros_like(heating[:, 0])]
    for level in range(levels - 1, 0, -1):
        lower.insert(0, lower[0] + heating[:, level])
    lower_local = jnp.stack(lower, axis=1)
    column_sum = jnp.sum(heating, axis=1)
    deeper = entering(column_sum, "lev", add_terms, jnp.zeros_like(column_sum))
    geopotential = surface[:, None, :] + deeper[:, None, :] + lower_local + 0.5 * heating
    total_levels = remap_level.shape[1]
    delta_col = (remap_level - jnp.arange(total_levels, dtype=jnp.int32)[None, :, None]).astype(
        jnp.float32
    )
    inputs = lax.all_to_all(
        jnp.stack([delta_col, remap_weight]), "lev", split_axis=2, concat_axis=3, tiled=True
    )
    margin = 4
    lev = lax.axis_index("lev")
    before = from_behind(field, "lev", 1)[:, :, levels - margin :]
    after = from_behind(field, "lev", -1)[:, :, :margin]
    before = jnp.where(lev == 0, field[:, :, :1], before)
    after = jnp.where(lev == lax.axis_size("lev") - 1, field[:, :, levels - 1 :], after)
    extended = jnp.concatenate([before, field, after], axis=2)
    remapped = local_parabola(extended, inputs[0][None], inputs[1][None])
    return (remapped, geopotential)


MARGIN = 4
FIRST_DOWN, LAST_UP, LAST_DOWN = 1, 0, 1
LANES = 128
SUB = 8
MESH = pl.DeviceIdType.MESH


def remote(src, dst, send, recv, axis, peer, other=None):
    return pltpu.make_async_remote_copy(
        src_ref=src,
        dst_ref=dst,
        send_sem=send,
        recv_sem=recv,
        device_id={axis: peer, **(other or {})},
        device_id_type=MESH,
    )


def starts(count):
    return [min(at, count - SUB) for at in range(0, count, SUB)]


def copy_rows(target, to, source, at, count):
    for s in starts(count):
        target[pl.ds(to + s, SUB), :] = source[pl.ds(at + s, SUB), :]


def kernel(lats, levs, *refs):
    (
        h_state,
        h_courant,
        h_offsets,
        h_thickness,
        h_surface,
        h_level,
        h_weight,
        out,
        geo,
        state,
        courant,
        offsets,
        thickness,
        surface,
        remap_level,
        remap_weight,
        pack,
        pack_c,
        work_c,
        work,
        mid,
        taps,
        ret,
        ext,
        rpack,
        rrecv,
        rall,
        delta,
        weight,
        thick,
        surf,
        hsum,
        psum,
        csum,
        sums,
        value,
        ins,
        fs,
        fr,
        bs,
        br,
        zs,
        zr,
        rs,
        rr,
        ps,
        pr,
        ss,
        sr,
        far,
        side,
    ) = refs
    count, rows, levels, width = state.shape
    cols = width // LANES
    band = rows * cols
    slab = band * lats
    room = work.shape[0] // count
    low = -(-2 * cols // SUB) * SUB
    deep = (levels + 2 * MARGIN) * band
    piece = remap_level.shape[2]
    plan = [
        (f >= count - LAST_UP, f < FIRST_DOWN or f >= count - LAST_DOWN) for f in range(count)
    ]
    cuts = [f for f in range(1, count) if f == 1 or plan[f] != plan[f - 1]]
    spans = list(zip([0, *cuts], [*cuts, count]))
    me = lax.axis_index("lat")
    lev = lax.axis_index("lev")
    core = lax.rem(lev, 2)
    if lats == 4:
        across = lax.rem(me + 2, lats)
        peers = [lats - 1 - me, across, lats - 1 - across]
    else:
        peers = [lax.rem(me + d, lats) for d in range(1, lats)]

    barrier = pltpu.get_barrier_semaphore()
    chips = levs // 2
    chip = lev // 2
    for peer in peers:
        pl.semaphore_signal(barrier, inc=1, device_id={"lat": peer}, device_id_type=MESH)
    pl.semaphore_signal(
        barrier, inc=1, device_id={"lev": lev + 1 - 2 * core}, device_id_type=MESH
    )

    def near(step):
        return jnp.logical_and(chip + step >= 0, chip + step < chips)

    for step in (-1, 1):
        for c in range(2):

            @pl.when(near(step))
            def _():
                pl.semaphore_signal(
                    barrier,
                    inc=1,
                    device_id={"lev": jnp.clip(2 * (chip + step) + c, 0, levs - 1)},
                    device_id_type=MESH,
                )

    loads = [
        pltpu.make_async_copy(a, b, ins.at[n])
        for n, (a, b) in enumerate(
            (
                (h_courant, courant),
                (h_offsets, offsets),
                (h_state, state),
                (h_level, remap_level),
                (h_weight, remap_weight),
                (h_thickness, thickness),
                (h_surface, surface),
            )
        )
    ]
    for c in loads:
        c.start()

    def spread(target, first, stride, tile, where):
        for c in range(cols):
            target[pl.ds(first + c, tile.shape[-2], stride=stride), :] = tile[
                (*where, slice(None), slice(c * LANES, (c + 1) * LANES))
            ]

    for c in loads[:3]:
        c.wait()
    for r in range(rows):
        for g in range(2):
            for c in range(cols):
                lanes = slice(c * LANES, (c + 1) * LANES)
                pack_c[pl.ds(g * band + r * cols + c, levels, stride=4 * band), :] = courant[
                    g, r, :, lanes
                ]
                pack_c[pl.ds((g + 2) * band + r * cols + c, levels, stride=4 * band), :] = offsets[
                    g, r, :, lanes
                ].astype(jnp.float32)
    for f in range(count):
        for r in range(rows):
            spread(pack, f * band + r * cols, count * band, state, (f, r))

    sides = (chip > 0).astype(jnp.int32) + (chip < chips - 1).astype(jnp.int32)
    pl.semaphore_wait(barrier, len(peers) + 1 + 2 * sides)

    def coefficient_copy(n):
        return [
            remote(
                pack_c.at[pl.ds((peers[n] * 4 + g) * band, band)],
                work_c.at[pl.ds(g * room + low + band * me, band)],
                fs.at[count + g, n],
                fr.at[count + g, n],
                "lat",
                peers[n],
            )
            for g in range(4)
        ]

    def field_copy(f, n):
        return remote(
            pack.at[pl.ds((peers[n] * count + f) * band, band)],
            work.at[pl.ds(f * room + low + band * me, band)],
            fs.at[f, n],
            fr.at[f, n],
            "lat",
            peers[n],
        )

    def back_copy(f, n):
        return remote(
            ret.at[pl.ds(f * slab + band * peers[n], band)],
            ext.at[pl.ds(f * deep + (MARGIN + me) * band, band)],
            bs.at[f, n],
            br.at[f, n],
            "lat",
            peers[n],
        )

    def level_copy(f, way, n):
        level = peers[n] if n < len(peers) else me
        target = ((0, MARGIN + levels)[way] + level) * band
        peer = (jnp.minimum(lev + 1, levs - 1), jnp.maximum(lev - 1, 0))[way]
        if n < len(peers):
            source = ext.at[pl.ds(f * deep + (MARGIN + level) * band, band)]
        else:
            source = ret.at[pl.ds(f * slab + level * band, band)]
        return remote(
            source,
            ext.at[pl.ds(f * deep + target, band)],
            zs.at[f, way, n],
            zr.at[f, way, n],
            "lev",
            peer,
        )

    def direct_copy(f, way, n):
        target = ((0, MARGIN + levels)[way] + me) * band
        peer = (jnp.minimum(lev + 1, levs - 1), jnp.maximum(lev - 1, 0))[way]
        return remote(
            ret.at[pl.ds(f * slab + band * peers[n], band)],
            ext.at[pl.ds(f * deep + target, band)],
            zs.at[f, way, n],
            zr.at[f, way, n],
            "lev",
            peer,
            {"lat": peers[n]},
        )

    up = jnp.logical_and(core == 1, lev < levs - 1)
    down = jnp.logical_and(core == 0, lev > 0)

    def direct_start(f, direct):
        for way, here in enumerate((up, down)):
            if direct[way]:

                @pl.when(here)
                def _():
                    for n in ways:
                        direct_copy(f, way, n).start()

    def level_start(f, n, direct):
        @pl.when(core == 0 if direct[0] else lev < levs - 1)
        def _():
            level_copy(f, 0, n).start()

        @pl.when(core == 1 if direct[1] else lev > 0)
        def _():
            level_copy(f, 1, n).start()

    def spread_remap(step):
        for c in range(2):
            if step or c:

                @pl.when(near(step))
                def _():
                    remap_copy(step, c).start()

    def remap_copy(step, c):
        n = chips - 1 + step
        to = jnp.clip(2 * (chip + step) + (c + core) % 2, 0, levs - 1)
        return remote(rpack.at[to], rrecv.at[lev], rs.at[n, c], rr.at[n, c], "lev", to)

    def remap_arrival(step, c):
        n = chips - 1 + step
        return remote(
            rpack.at[lev], rrecv.at[lev], rs.at[n, c], rr.at[n, c], "lev", lev + 1 - 2 * core
        )

    def relay(way, hop):
        step = (1, -1)[way]

        @pl.when(jnp.logical_and(near(step), near(-step * hop)))
        def _():
            pl.semaphore_signal(
                far.at[way, hop],
                inc=1,
                device_id={"lev": jnp.clip(lev + 2 * step, 0, levs - 1)},
                device_id_type=MESH,
            )

    held = pl.ds(0, band)

    def pair_copy():
        return remote(hsum.at[held], psum.at[held], ps, pr, "lev", lev + 1 - 2 * core)

    def sum_copy(d):
        return remote(csum.at[held], sums.at[d, held], ss.at[d], sr.at[d], "lev", jnp.maximum(lev - 2 * d, core))

    def far_copy(c):
        at, to = chips - 1, jnp.maximum(2 * (chip - chips + 1), 0) + (c + core) % 2
        return remote(hsum.at[held], sums.at[at + core, held], ss.at[at + c], sr.at[at + core], "lev", to)

    def far_arrival(c):
        at = chips - 1 + c
        return remote(hsum.at[held], sums.at[at, held], ss.at[at], sr.at[at], "lev", lev + 1 - 2 * core)

    ways = range(len(peers))
    for way in range(2):
        relay(way, 1)
    for n in ways:
        pl.semaphore_signal(
            side.at[n], inc=1, device_id={"lat": peers[n]}, device_id_type=MESH
        )
    for n in ways:
        for c in coefficient_copy(n):
            c.start()
    for f in range(count):
        for n in ways:
            field_copy(f, n).start()

    for c in loads[3:]:
        c.wait()
    for p in range(levs):
        for r in range(rows):
            lo = p * levels
            ks = lo + lax.broadcasted_iota(jnp.int32, (levels, piece), 0)
            rpack[p, 0, r] = (remap_level[r, lo : lo + levels, :] - ks).astype(jnp.float32)
            rpack[p, 1, r] = remap_weight[r, lo : lo + levels, :]
    for r in range(rows):
        spread(thick, r * cols, band, thickness, (r,))
    spread(surf, 0, cols, surface, ())
    blank = jnp.zeros((SUB, LANES), jnp.float32)
    edges = [min(at, room - SUB) for at in (*range(0, low, SUB), *range(low + slab, room, SUB))]
    for f in range(count):
        copy_rows(work, f * room + low + band * me, pack, (me * count + f) * band, band)
        for at in edges:
            work[pl.ds(f * room + at, SUB), :] = blank
    for at in edges:
        mid[pl.ds(at, SUB), :] = blank
        for g in range(4):
            work_c[pl.ds(g * room + at, SUB), :] = blank
    for g in range(4):
        copy_rows(work_c, g * room + low + band * me, pack_c, (me * 4 + g) * band, band)
    rrecv[lev] = rpack[lev]
    for step in (-1, 0, 1):
        spread_remap(step)
    for hop in range(1, chips - 1):
        for way in range(2):
            back = -(hop + 1) if way == 0 else hop + 1

            @pl.when(near(back))
            def _():
                pl.semaphore_wait(far.at[way, hop], 1)

            if hop + 1 < chips - 1:
                relay(way, hop + 1)
            spread_remap(back)

    row = lax.broadcasted_iota(jnp.int32, (SUB, LANES), 0)
    lane = lax.broadcasted_iota(jnp.int32, (SUB, LANES), 1)
    masks = {1: lane == LANES - 1, 2: lane >= LANES - 2, -1: lane < 1, -2: lane < 2}

    def beside(source, base, p, here, shifts):
        found = []
        for way in (1, -1):
            some = [s for s in shifts if s * way > 0]
            if not some:
                continue
            near_by = source[pl.ds(base + p - way, SUB), :]
            at = (-p if way == 1 else cols - 1 - p) % cols
            if at < SUB:
                wrapped = source[pl.ds(base + p - way + way * cols, SUB), :]
                near_by = jnp.where(row == at, wrapped, near_by)
            for s in some:
                mixed = jnp.where(masks[s], near_by, here)
                found.append(pltpu.roll(mixed, s % LANES, 1))
        return found

    def substep(source, base, target, to):
        for p in starts(slab):
            here = source[pl.ds(base + p, SUB), :]
            terms = [here, *beside(source, base, p, here, (1, 2, -1, -2))]
            terms += [source[pl.ds(base + p + d * cols, SUB), :] for d in (-1, -2, 1, 2)]
            products = [taps[pl.ds(g * slab + p, SUB), :] * q for g, q in enumerate(terms)]
            while len(products) > 1:
                pairs = [x + y for x, y in zip(products[::2], products[1::2])]
                products = pairs + products[2 * len(pairs) :]
            target[pl.ds(to + p, SUB), :] = products[0]

    for n in ways:
        for c in coefficient_copy(n):
            c.wait_recv()
    none = jnp.zeros((SUB, LANES), jnp.float32)
    for p in starts(slab):
        c0, c1, o0, o1 = (work_c[pl.ds(g * room + low + p, SUB), :] for g in range(4))
        under, under_o = (work_c[pl.ds(g * room + low + p - cols, SUB), :] for g in (0, 2))
        back, back_o = (
            beside(work_c, g * room + low, p, here, (1,))[0] for g, here in ((1, c1), (3, o1))
        )
        middle = none + 1.0
        for first, near_c, near_o, far_c, far_o in ((1, c1, o1, back, back_o), (5, c0, o0, under, under_o)):
            own = [jnp.where(near_o == float(o), near_c, none) for o in range(-1, 3)]
            other = [jnp.where(far_o == float(o), far_c, none) for o in range(-1, 3)]
            middle = middle + (other[2] - own[1])
            for g, tap in enumerate((other[1] - own[0], other[0], other[3] - own[2], -own[3])):
                taps[pl.ds((first + g) * slab + p, SUB), :] = tap
        taps[pl.ds(p, SUB), :] = middle

    def advect(f, direct):
        for n in ways:
            field_copy(f, n).wait_recv()
        substep(work, f * room + low, mid, low)
        substep(mid, low, ret, f * slab)
        direct_start(f, direct)
        for n in ways:
            back_copy(f, n).start()
        level_start(f, len(peers), (False, False))
        copy_rows(ext, f * deep + (MARGIN + me) * band, ret, f * slab + band * me, band)

    def loop(first, end, body, *rest):
        def step(f, carry):
            body(f, *rest)
            return carry

        lax.fori_loop(first, end, step, 0)

    for n in ways:
        pl.semaphore_wait(side.at[n], 1)
    for start, end in spans:
        loop(start, end, advect, plan[start])

    for n in ways:
        for c in coefficient_copy(n):
            c.wait_send()
        for f in range(count):
            field_copy(f, n).wait_send()
    for step in range(1 - chips, chips):
        for c in range(2):
            if step or c:

                @pl.when(near(-step))
                def _():
                    remap_arrival(step, c).wait_recv()

                @pl.when(near(step))
                def _():
                    remap_copy(step, c).wait_send()

    for p in range(levs):
        rall[:, :, :, p * piece : (p + 1) * piece] = rrecv[p]
    for g, target in enumerate((delta, weight)):
        for r in range(rows):
            spread(target, r * cols, band, rall, (g, r))

    def heat(k, s):
        at = ext[pl.ds((MARGIN + k) * band + s, SUB), :]
        return at * thick[pl.ds(k * band + s, SUB), :]

    def share(f, direct):
        for n in reversed(ways):
            back_copy(f, n).wait_recv()
            level_start(f, n, direct)

    def sent(f):
        for n in ways:
            back_copy(f, n).wait_send()

    for n in ways:
        back_copy(0, n).wait_recv()
    for s in starts(band):
        hsum[pl.ds(s, SUB), :] = functools.reduce(add_terms, [heat(k, s) for k in range(levels)])

    @pl.when(chip == chips - 1)
    def _():
        for c in range(2):
            far_copy(c).start()

    pair_copy().start()
    for n in ways:
        level_start(0, n, plan[0])
    pair_copy().wait_recv()
    for s in starts(band):
        csum[pl.ds(s, SUB), :] = hsum[pl.ds(s, SUB), :] + psum[pl.ds(s, SUB), :]
    for d in range(1, chips - 1):

        @pl.when(chip >= d)
        def _():
            sum_copy(d).start()

    for start, end in spans[1:]:
        loop(start, end, share, plan[start])
    loop(0, count, sent)

    def remap(f):
        base = f * deep

        @pl.when(lev > 0)
        def _():
            for n in range(lats):
                level_copy(f, 0, n).wait_recv()
                level_copy(f, 1, n).wait_send()

        @pl.when(lev < levs - 1)
        def _():
            for n in range(lats):
                level_copy(f, 1, n).wait_recv()
                level_copy(f, 0, n).wait_send()

        @pl.when(lev == 0)
        def _():
            for m in range(MARGIN):
                copy_rows(ext, base + m * band, ext, base + MARGIN * band, band)

        @pl.when(lev == levs - 1)
        def _():
            end = base + (MARGIN + levels) * band
            for m in range(MARGIN):
                copy_rows(ext, end + m * band, ext, end - band, band)

        for s in starts(band):
            q = [ext[pl.ds(base + m * band + s, SUB), :] for m in range(levels + 2 * MARGIN)]
            edge = {
                m: (7.0 * (q[m - 1] + q[m]) - (q[m - 2] + q[m + 1])) * (1.0 / 12.0)
                for m in range(2, levels + 2 * MARGIN - 1)
            }
            for k in range(levels):
                dk = delta[pl.ds(k * band + s, SUB), :]
                wk = weight[pl.ds(k * band + s, SUB), :]
                at = k + MARGIN
                centre, left, right = q[at - 2], edge[at - 2], edge[at - 1]
                for o in range(-1, 3):
                    chosen = dk == float(o)
                    centre = jnp.where(chosen, q[at + o], centre)
                    left = jnp.where(chosen, edge[at + o], left)
                    right = jnp.where(chosen, edge[at + o + 1], right)
                curve = 6.0 * centre - 3.0 * (left + right)
                value[pl.ds(k * band + s, SUB), :] = left + wk * (
                    (right - left) + curve * (1.0 - wk)
                )
        for r in range(rows):
            for c in range(cols):
                out[f, r, :, c * LANES : (c + 1) * LANES] = value[
                    pl.ds(r * cols + c, levels, stride=band), :
                ]

    loop(0, count, remap)
    for d in range(1, chips - 1):

        @pl.when(chip + d < chips)
        def _():
            sum_copy(d).wait_recv()

    @pl.when(chip == 0)
    def _():
        for c in range(2):
            far_arrival(c).wait_recv()

    for s in starts(band):
        below = surf[pl.ds(s, SUB), :]
        for here, more in (
            (core == 0, psum[pl.ds(s, SUB), :]),
            *((chip + d < chips, sums[d, pl.ds(s, SUB), :]) for d in range(1, chips - 1)),
            *((chip == 0, sums[chips - 1 + c, pl.ds(s, SUB), :]) for c in range(2)),
        ):
            below = below + jnp.where(here, more, jnp.zeros_like(more))
        for k in range(levels - 1, -1, -1):
            term = heat(k, s)
            value[pl.ds(k * band + s, SUB), :] = below + 0.5 * term
            below = below + term
    for r in range(rows):
        for c in range(cols):
            geo[r, :, c * LANES : (c + 1) * LANES] = value[
                pl.ds(r * cols + c, levels, stride=band), :
            ]

    pair_copy().wait_send()

    @pl.when(chip == chips - 1)
    def _():
        for c in range(2):
            far_copy(c).wait_send()

    for d in range(1, chips - 1):

        @pl.when(chip >= d)
        def _():
            sum_copy(d).wait_send()


def leave(out, geo, h_out, h_geo, sems):
    copies = [
        pltpu.make_async_copy(a, b, sems.at[n])
        for n, (a, b) in enumerate(((out, h_out), (geo, h_geo)))
    ]
    for c in copies:
        c.start()
    for c in copies:
        c.wait()


def fused(lats, levs, *args):
    state, courant, offsets, thickness, surface, level, weight = args
    count, rows, levels, width = state.shape
    piece = level.shape[2]
    cols = width // LANES
    band = rows * cols
    slab = band * lats
    room = -(-(slab + 2 * (-(-2 * cols // SUB) * SUB)) // SUB) * SUB
    f32 = jnp.float32
    dma = pltpu.SemaphoreType.DMA

    def tall(n):
        return pltpu.VMEM((-(-n // SUB) * SUB, LANES), f32)

    results = pl.pallas_call(
        functools.partial(kernel, lats, levs),
        out_shape=(pltpu.VMEM(state.shape, f32), pltpu.VMEM(thickness.shape, f32)),
        in_specs=[pl.BlockSpec(memory_space=pl.ANY)] * 7,
        scratch_shapes=[
            *(pltpu.VMEM(x.shape, x.dtype) for x in args),
            tall(levels * count * band),
            tall(levels * 4 * band),
            tall(4 * room),
            tall(count * room),
            tall(room),
            tall(9 * slab),
            tall(count * slab),
            tall(count * (levels + 2 * MARGIN) * band),
            pltpu.VMEM((levs, 2, rows, levels, piece), f32),
            pltpu.VMEM((levs, 2, rows, levels, piece), f32),
            pltpu.VMEM((2, rows, levels, width), f32),
            tall(levels * band),
            tall(levels * band),
            tall(levels * band),
            tall(band),
            tall(band),
            tall(band),
            tall(band),
            pltpu.VMEM((levs // 2 + 1, -(-band // SUB) * SUB, LANES), f32),
            tall(levels * band),
            dma((7,)),
            dma((count + 4, lats)),
            dma((count + 4, lats)),
            dma((count, lats)),
            dma((count, lats)),
            dma((count, 2, lats)),
            dma((count, 2, lats)),
            dma((levs, 2)),
            dma((levs, 2)),
            dma,
            dma,
            dma((levs // 2 + 1,)),
            dma((levs // 2 + 1,)),
            pltpu.SemaphoreType.REGULAR((2, levs // 2)),
            pltpu.SemaphoreType.REGULAR((lats,)),
        ],
        compiler_params=pltpu.CompilerParams(collective_id=0, has_side_effects=True),
    )(*args)
    results = [pltpu.with_memory_space_constraint(x, pltpu.VMEM) for x in results]
    return pl.pallas_call(
        leave,
        out_shape=tuple(pltpu.HBM(x.shape, x.dtype) for x in results),
        in_specs=[pl.BlockSpec(memory_space=pltpu.VMEM)] * 2,
        out_specs=(pl.BlockSpec(memory_space=pltpu.HBM),) * 2,
        scratch_shapes=[dma((2,))],
    )(*results)


def solution(mesh):
    in_specs = (
        P(None, "lat", "lev", None),
        P(None, "lat", "lev", None),
        P(None, "lat", "lev", None),
        P("lat", "lev", None),
        P("lat", None),
        P("lat", None, "lev"),
        P("lat", None, "lev"),
    )
    out_specs = (P(None, "lat", "lev", None), P("lat", "lev", None))
    lats, levs = mesh.shape["lat"], mesh.shape["lev"]

    def body(state, *rest):
        count, rows, levels, width = state.shape
        small = width % LANES or rows * (width // LANES) < SUB
        if levels != lats or levels != MARGIN or small or levs % 2 or levs < 4 or count < 2:
            return per_device(state, *rest)
        return fused(lats, levs, state, *rest)

    return jax.shard_map(
        body, mesh=mesh, in_specs=in_specs, out_specs=out_specs, check_vma=False
    )
```

```python
import functools

import jax
import jax.numpy as jnp
from jax import lax
from jax.experimental import pallas as pl
from jax.experimental.pallas import tpu as pltpu
from jax.sharding import PartitionSpec as P

SUBSTEPS = 2


def extended_2(block, sides, width):
    for axis, dim in sides:
        count = lax.axis_size(axis)
        forward = [(i, i + 1) for i in range(count - 1)]
        backward = [(target, source) for source, target in forward]
        low = lax.ppermute(
            lax.slice_in_dim(block, block.shape[dim] - width, None, axis=dim), axis, forward
        )
        high = lax.ppermute(lax.slice_in_dim(block, 0, width, axis=dim), axis, backward)
        block = jnp.concatenate([low, block, high], axis=dim)
    return block


def from_behind(x, axis, by):
    count = lax.axis_size(axis)
    pairs = [(i, i + by) for i in range(count) if 0 <= i + by < count]
    return lax.ppermute(x, axis, pairs)


def entering(x, axis, combine, identity):
    count, position = (lax.axis_size(axis), lax.axis_index(axis))
    everything = lax.all_gather(x, axis)
    start = jnp.broadcast_to(jnp.asarray(identity, x.dtype), x.shape)

    def lap(k, before):
        at = count - 1 - k
        reached = at > position
        new = combine(before, everything[at])
        return jnp.where(reached, new, before)

    return lax.fori_loop(0, count, lap, start)


def local_parabola(extended, delta, weight):
    margin = 4
    count = extended.shape[-2] - 2 * margin
    edges = (
        7.0 * (extended[..., 1:-2, :] + extended[..., 2:-1, :])
        - (extended[..., :-3, :] + extended[..., 3:, :])
    ) / 12.0
    centre = jnp.zeros(extended.shape[:-2] + (count, extended.shape[-1]), jnp.float32)
    left = centre
    right = centre
    for offset in range(-2, 3):
        chosen = delta == offset
        start = margin + offset
        centre = jnp.where(chosen, extended[..., start : start + count, :], centre)
        left = jnp.where(chosen, edges[..., start - 2 : start - 2 + count, :], left)
        right = jnp.where(chosen, edges[..., start - 1 : start - 1 + count, :], right)
    slope = right - left
    curve = 6.0 * centre - 3.0 * (left + right)
    return left + weight * (slope + curve * (1.0 - weight))


def add_terms(earlier, later):
    return earlier + later


def per_device(state, courant, offsets, log_thickness, surface, remap_level, remap_weight):
    count, rows, levels, width = state.shape
    north_masks = [offsets[0] == offset for offset in range(-1, 3)]
    east_masks = [offsets[1] == offset for offset in range(-1, 3)]
    field = state
    for substep in range(SUBSTEPS):
        padded = extended_2(field, (("lat", 1),), 2)
        picked = jnp.zeros_like(field)
        for number, offset in enumerate(range(-1, 3)):
            picked = jnp.where(
                north_masks[number][None], padded[:, offset + 2 : offset + 2 + rows], picked
            )
        north = courant[0][None] * picked
        below = from_behind(north[:, rows - 1 :], "lat", 1)
        south = jnp.concatenate([below, north[:, : rows - 1]], axis=1)
        moved = jnp.zeros_like(field)
        for number, offset in enumerate(range(-1, 3)):
            moved = jnp.where(east_masks[number][None], jnp.roll(field, -offset, axis=3), moved)
        east = courant[1][None] * moved
        west = jnp.roll(east, 1, axis=3)
        field = field - (north - south) - (east - west)
    heating = field[0] * log_thickness
    lower = [jnp.zeros_like(heating[:, 0])]
    for level in range(levels - 1, 0, -1):
        lower.insert(0, lower[0] + heating[:, level])
    lower_local = jnp.stack(lower, axis=1)
    column_sum = jnp.sum(heating, axis=1)
    deeper = entering(column_sum, "lev", add_terms, jnp.zeros_like(column_sum))
    geopotential = surface[:, None, :] + deeper[:, None, :] + lower_local + 0.5 * heating
    total_levels = remap_level.shape[1]
    delta_col = (remap_level - jnp.arange(total_levels, dtype=jnp.int32)[None, :, None]).astype(
        jnp.float32
    )
    inputs = lax.all_to_all(
        jnp.stack([delta_col, remap_weight]), "lev", split_axis=2, concat_axis=3, tiled=True
    )
    margin = 4
    lev = lax.axis_index("lev")
    before = from_behind(field, "lev", 1)[:, :, levels - margin :]
    after = from_behind(field, "lev", -1)[:, :, :margin]
    before = jnp.where(lev == 0, field[:, :, :1], before)
    after = jnp.where(lev == lax.axis_size("lev") - 1, field[:, :, levels - 1 :], after)
    extended = jnp.concatenate([before, field, after], axis=2)
    remapped = local_parabola(extended, inputs[0][None], inputs[1][None])
    return (remapped, geopotential)


MARGIN = 4
FIRST_DOWN, LAST_UP, LAST_DOWN = 1, 0, 4
LANES = 128
SUB = 8
MESH = pl.DeviceIdType.MESH


def remote(src, dst, send, recv, axis, peer, other=None):
    return pltpu.make_async_remote_copy(
        src_ref=src,
        dst_ref=dst,
        send_sem=send,
        recv_sem=recv,
        device_id={axis: peer, **(other or {})},
        device_id_type=MESH,
    )


def starts(count):
    return [min(at, count - SUB) for at in range(0, count, SUB)]


def copy_rows(target, to, source, at, count):
    for s in starts(count):
        target[pl.ds(to + s, SUB), :] = source[pl.ds(at + s, SUB), :]


def kernel(lats, levs, *refs):
    (
        h_state,
        h_courant,
        h_offsets,
        h_thickness,
        h_surface,
        h_level,
        h_weight,
        out,
        geo,
        state,
        courant,
        offsets,
        thickness,
        surface,
        remap_level,
        remap_weight,
        pack,
        pack_c,
        work_c,
        work,
        mid,
        taps,
        ret,
        ext,
        rpack,
        rrecv,
        rall,
        delta,
        weight,
        thick,
        surf,
        hsum,
        psum,
        csum,
        sums,
        value,
        ins,
        fs,
        fr,
        bs,
        br,
        zs,
        zr,
        rs,
        rr,
        ps,
        pr,
        ss,
        sr,
        far,
        side,
    ) = refs
    count, rows, levels, width = state.shape
    cols = width // LANES
    band = rows * cols
    slab = band * lats
    room = work.shape[0] // count
    low = -(-2 * cols // SUB) * SUB
    deep = (levels + 2 * MARGIN) * band
    piece = remap_level.shape[2]
    plan = [
        (f >= count - LAST_UP, f < FIRST_DOWN or f >= count - LAST_DOWN) for f in range(count)
    ]
    cuts = [f for f in range(1, count) if f == 1 or plan[f] != plan[f - 1]]
    spans = list(zip([0, *cuts], [*cuts, count]))
    me = lax.axis_index("lat")
    lev = lax.axis_index("lev")
    core = lax.rem(lev, 2)
    if lats == 4:
        across = lax.rem(me + 2, lats)
        peers = [lats - 1 - me, across, lats - 1 - across]
    else:
        peers = [lax.rem(me + d, lats) for d in range(1, lats)]

    barrier = pltpu.get_barrier_semaphore()
    chips = levs // 2
    chip = lev // 2
    for peer in peers:
        pl.semaphore_signal(barrier, inc=1, device_id={"lat": peer}, device_id_type=MESH)
    pl.semaphore_signal(
        barrier, inc=1, device_id={"lev": lev + 1 - 2 * core}, device_id_type=MESH
    )

    def near(step):
        return jnp.logical_and(chip + step >= 0, chip + step < chips)

    for step in (-1, 1):
        for c in range(2):

            @pl.when(near(step))
            def _():
                pl.semaphore_signal(
                    barrier,
                    inc=1,
                    device_id={"lev": jnp.clip(2 * (chip + step) + c, 0, levs - 1)},
                    device_id_type=MESH,
                )

    loads = [
        pltpu.make_async_copy(a, b, ins.at[n])
        for n, (a, b) in enumerate(
            (
                (h_courant, courant),
                (h_offsets, offsets),
                (h_state, state),
                (h_level, remap_level),
                (h_weight, remap_weight),
                (h_thickness, thickness),
                (h_surface, surface),
            )
        )
    ]
    for c in loads:
        c.start()

    def spread(target, first, stride, tile, where):
        for c in range(cols):
            target[pl.ds(first + c, tile.shape[-2], stride=stride), :] = tile[
                (*where, slice(None), slice(c * LANES, (c + 1) * LANES))
            ]

    for c in loads[:3]:
        c.wait()
    for r in range(rows):
        for g in range(2):
            for c in range(cols):
                lanes = slice(c * LANES, (c + 1) * LANES)
                pack_c[pl.ds(g * band + r * cols + c, levels, stride=4 * band), :] = courant[
                    g, r, :, lanes
                ]
                pack_c[pl.ds((g + 2) * band + r * cols + c, levels, stride=4 * band), :] = offsets[
                    g, r, :, lanes
                ].astype(jnp.float32)
    for f in range(count):
        for r in range(rows):
            spread(pack, f * band + r * cols, count * band, state, (f, r))

    sides = (chip > 0).astype(jnp.int32) + (chip < chips - 1).astype(jnp.int32)
    pl.semaphore_wait(barrier, len(peers) + 1 + 2 * sides)

    def coefficient_copy(n):
        return [
            remote(
                pack_c.at[pl.ds((peers[n] * 4 + g) * band, band)],
                work_c.at[pl.ds(g * room + low + band * me, band)],
                fs.at[count + g, n],
                fr.at[count + g, n],
                "lat",
                peers[n],
            )
            for g in range(4)
        ]

    def field_copy(f, n):
        return remote(
            pack.at[pl.ds((peers[n] * count + f) * band, band)],
            work.at[pl.ds(f * room + low + band * me, band)],
            fs.at[f, n],
            fr.at[f, n],
            "lat",
            peers[n],
        )

    def back_copy(f, n):
        return remote(
            ret.at[pl.ds(f * slab + band * peers[n], band)],
            ext.at[pl.ds(f * deep + (MARGIN + me) * band, band)],
            bs.at[f, n],
            br.at[f, n],
            "lat",
            peers[n],
        )

    def level_copy(f, way, n):
        level = peers[n] if n < len(peers) else me
        target = ((0, MARGIN + levels)[way] + level) * band
        peer = (jnp.minimum(lev + 1, levs - 1), jnp.maximum(lev - 1, 0))[way]
        if n < len(peers):
            source = ext.at[pl.ds(f * deep + (MARGIN + level) * band, band)]
        else:
            source = ret.at[pl.ds(f * slab + level * band, band)]
        return remote(
            source,
            ext.at[pl.ds(f * deep + target, band)],
            zs.at[f, way, n],
            zr.at[f, way, n],
            "lev",
            peer,
        )

    def direct_copy(f, way, n):
        target = ((0, MARGIN + levels)[way] + me) * band
        peer = (jnp.minimum(lev + 1, levs - 1), jnp.maximum(lev - 1, 0))[way]
        return remote(
            ret.at[pl.ds(f * slab + band * peers[n], band)],
            ext.at[pl.ds(f * deep + target, band)],
            zs.at[f, way, n],
            zr.at[f, way, n],
            "lev",
            peer,
            {"lat": peers[n]},
        )

    up = jnp.logical_and(core == 1, lev < levs - 1)
    down = jnp.logical_and(core == 0, lev > 0)

    def direct_start(f, direct):
        for way, here in enumerate((up, down)):
            if direct[way]:

                @pl.when(here)
                def _():
                    for n in ways:
                        direct_copy(f, way, n).start()

    def level_start(f, n, direct):
        @pl.when(core == 0 if direct[0] else lev < levs - 1)
        def _():
            level_copy(f, 0, n).start()

        @pl.when(core == 1 if direct[1] else lev > 0)
        def _():
            level_copy(f, 1, n).start()

    def spread_remap(step):
        for c in range(2):
            if step or c:

                @pl.when(near(step))
                def _():
                    remap_copy(step, c).start()

    def remap_copy(step, c):
        n = chips - 1 + step
        to = jnp.clip(2 * (chip + step) + (c + core) % 2, 0, levs - 1)
        return remote(rpack.at[to], rrecv.at[lev], rs.at[n, c], rr.at[n, c], "lev", to)

    def remap_arrival(step, c):
        n = chips - 1 + step
        return remote(
            rpack.at[lev], rrecv.at[lev], rs.at[n, c], rr.at[n, c], "lev", lev + 1 - 2 * core
        )

    def relay(way, hop):
        step = (1, -1)[way]

        @pl.when(jnp.logical_and(near(step), near(-step * hop)))
        def _():
            pl.semaphore_signal(
                far.at[way, hop],
                inc=1,
                device_id={"lev": jnp.clip(lev + 2 * step, 0, levs - 1)},
                device_id_type=MESH,
            )

    held = pl.ds(0, band)

    def pair_copy():
        return remote(hsum.at[held], psum.at[held], ps, pr, "lev", lev + 1 - 2 * core)

    def sum_copy(d):
        return remote(csum.at[held], sums.at[d, held], ss.at[d], sr.at[d], "lev", jnp.maximum(lev - 2 * d, core))

    def far_copy(c):
        at, to = chips - 1, jnp.maximum(2 * (chip - chips + 1), 0) + (c + core) % 2
        return remote(hsum.at[held], sums.at[at + core, held], ss.at[at + c], sr.at[at + core], "lev", to)

    def far_arrival(c):
        at = chips - 1 + c
        return remote(hsum.at[held], sums.at[at, held], ss.at[at], sr.at[at], "lev", lev + 1 - 2 * core)

    ways = range(len(peers))
    for way in range(2):
        relay(way, 1)
    for n in ways:
        pl.semaphore_signal(
            side.at[n], inc=1, device_id={"lat": peers[n]}, device_id_type=MESH
        )
    for n in ways:
        for c in coefficient_copy(n):
            c.start()
    for f in range(count):
        for n in ways:
            field_copy(f, n).start()

    for c in loads[3:]:
        c.wait()
    for p in range(levs):
        for r in range(rows):
            lo = p * levels
            ks = lo + lax.broadcasted_iota(jnp.int32, (levels, piece), 0)
            rpack[p, 0, r] = (remap_level[r, lo : lo + levels, :] - ks).astype(jnp.float32)
            rpack[p, 1, r] = remap_weight[r, lo : lo + levels, :]
    for r in range(rows):
        spread(thick, r * cols, band, thickness, (r,))
    spread(surf, 0, cols, surface, ())
    blank = jnp.zeros((SUB, LANES), jnp.float32)
    edges = [min(at, room - SUB) for at in (*range(0, low, SUB), *range(low + slab, room, SUB))]
    for f in range(count):
        copy_rows(work, f * room + low + band * me, pack, (me * count + f) * band, band)
        for at in edges:
            work[pl.ds(f * room + at, SUB), :] = blank
    for at in edges:
        mid[pl.ds(at, SUB), :] = blank
        for g in range(4):
            work_c[pl.ds(g * room + at, SUB), :] = blank
    for g in range(4):
        copy_rows(work_c, g * room + low + band * me, pack_c, (me * 4 + g) * band, band)
    rrecv[lev] = rpack[lev]
    for step in (-1, 0, 1):
        spread_remap(step)
    for hop in range(1, chips - 1):
        for way in range(2):
            back = -(hop + 1) if way == 0 else hop + 1

            @pl.when(near(back))
            def _():
                pl.semaphore_wait(far.at[way, hop], 1)

            if hop + 1 < chips - 1:
                relay(way, hop + 1)
            spread_remap(back)

    row = lax.broadcasted_iota(jnp.int32, (SUB, LANES), 0)
    lane = lax.broadcasted_iota(jnp.int32, (SUB, LANES), 1)
    masks = {1: lane == LANES - 1, 2: lane >= LANES - 2, -1: lane < 1, -2: lane < 2}

    def beside(source, base, p, here, shifts):
        found = []
        for way in (1, -1):
            some = [s for s in shifts if s * way > 0]
            if not some:
                continue
            near_by = source[pl.ds(base + p - way, SUB), :]
            at = (-p if way == 1 else cols - 1 - p) % cols
            if at < SUB:
                wrapped = source[pl.ds(base + p - way + way * cols, SUB), :]
                near_by = jnp.where(row == at, wrapped, near_by)
            for s in some:
                mixed = jnp.where(masks[s], near_by, here)
                found.append(pltpu.roll(mixed, s % LANES, 1))
        return found

    def substep(source, base, target, to):
        for p in starts(slab):
            here = source[pl.ds(base + p, SUB), :]
            terms = [here, *beside(source, base, p, here, (1, 2, -1, -2))]
            terms += [source[pl.ds(base + p + d * cols, SUB), :] for d in (-1, -2, 1, 2)]
            products = [taps[pl.ds(g * slab + p, SUB), :] * q for g, q in enumerate(terms)]
            while len(products) > 1:
                pairs = [x + y for x, y in zip(products[::2], products[1::2])]
                products = pairs + products[2 * len(pairs) :]
            target[pl.ds(to + p, SUB), :] = products[0]

    for n in ways:
        for c in coefficient_copy(n):
            c.wait_recv()
    none = jnp.zeros((SUB, LANES), jnp.float32)
    for p in starts(slab):
        c0, c1, o0, o1 = (work_c[pl.ds(g * room + low + p, SUB), :] for g in range(4))
        under, under_o = (work_c[pl.ds(g * room + low + p - cols, SUB), :] for g in (0, 2))
        back, back_o = (
            beside(work_c, g * room + low, p, here, (1,))[0] for g, here in ((1, c1), (3, o1))
        )
        middle = none + 1.0
        for first, near_c, near_o, far_c, far_o in ((1, c1, o1, back, back_o), (5, c0, o0, under, under_o)):
            own = [jnp.where(near_o == float(o), near_c, none) for o in range(-1, 3)]
            other = [jnp.where(far_o == float(o), far_c, none) for o in range(-1, 3)]
            middle = middle + (other[2] - own[1])
            for g, tap in enumerate((other[1] - own[0], other[0], other[3] - own[2], -own[3])):
                taps[pl.ds((first + g) * slab + p, SUB), :] = tap
        taps[pl.ds(p, SUB), :] = middle

    def advect(f, direct):
        for n in ways:
            field_copy(f, n).wait_recv()
        substep(work, f * room + low, mid, low)
        substep(mid, low, ret, f * slab)
        direct_start(f, direct)
        for n in ways:
            back_copy(f, n).start()
        level_start(f, len(peers), (False, False))
        copy_rows(ext, f * deep + (MARGIN + me) * band, ret, f * slab + band * me, band)

    def loop(first, end, body, *rest):
        def step(f, carry):
            body(f, *rest)
            return carry

        lax.fori_loop(first, end, step, 0)

    for n in ways:
        pl.semaphore_wait(side.at[n], 1)
    for start, end in spans:
        loop(start, end, advect, plan[start])

    for n in ways:
        for c in coefficient_copy(n):
            c.wait_send()
        for f in range(count):
            field_copy(f, n).wait_send()
    for step in range(1 - chips, chips):
        for c in range(2):
            if step or c:

                @pl.when(near(-step))
                def _():
                    remap_arrival(step, c).wait_recv()

                @pl.when(near(step))
                def _():
                    remap_copy(step, c).wait_send()

    for p in range(levs):
        rall[:, :, :, p * piece : (p + 1) * piece] = rrecv[p]
    for g, target in enumerate((delta, weight)):
        for r in range(rows):
            spread(target, r * cols, band, rall, (g, r))

    def heat(k, s):
        at = ext[pl.ds((MARGIN + k) * band + s, SUB), :]
        return at * thick[pl.ds(k * band + s, SUB), :]

    def share(f, direct):
        for n in reversed(ways):
            back_copy(f, n).wait_recv()
            level_start(f, n, direct)

    def sent(f):
        for n in ways:
            back_copy(f, n).wait_send()

    for n in ways:
        back_copy(0, n).wait_recv()
    for s in starts(band):
        hsum[pl.ds(s, SUB), :] = functools.reduce(add_terms, [heat(k, s) for k in range(levels)])

    @pl.when(chip == chips - 1)
    def _():
        for c in range(2):
            far_copy(c).start()

    pair_copy().start()
    for n in ways:
        level_start(0, n, plan[0])
    pair_copy().wait_recv()
    for s in starts(band):
        csum[pl.ds(s, SUB), :] = hsum[pl.ds(s, SUB), :] + psum[pl.ds(s, SUB), :]
    for d in range(1, chips - 1):

        @pl.when(chip >= d)
        def _():
            sum_copy(d).start()

    for start, end in spans[1:]:
        loop(start, end, share, plan[start])
    loop(0, count, sent)

    def remap(f):
        base = f * deep

        @pl.when(lev > 0)
        def _():
            for n in range(lats):
                level_copy(f, 0, n).wait_recv()
                level_copy(f, 1, n).wait_send()

        @pl.when(lev < levs - 1)
        def _():
            for n in range(lats):
                level_copy(f, 1, n).wait_recv()
                level_copy(f, 0, n).wait_send()

        @pl.when(lev == 0)
        def _():
            for m in range(MARGIN):
                copy_rows(ext, base + m * band, ext, base + MARGIN * band, band)

        @pl.when(lev == levs - 1)
        def _():
            end = base + (MARGIN + levels) * band
            for m in range(MARGIN):
                copy_rows(ext, end + m * band, ext, end - band, band)

        for s in starts(band):
            q = [ext[pl.ds(base + m * band + s, SUB), :] for m in range(levels + 2 * MARGIN)]
            edge = {
                m: (7.0 * (q[m - 1] + q[m]) - (q[m - 2] + q[m + 1])) * (1.0 / 12.0)
                for m in range(2, levels + 2 * MARGIN - 1)
            }
            for k in range(levels):
                dk = delta[pl.ds(k * band + s, SUB), :]
                wk = weight[pl.ds(k * band + s, SUB), :]
                at = k + MARGIN
                centre, left, right = q[at - 2], edge[at - 2], edge[at - 1]
                for o in range(-1, 3):
                    chosen = dk == float(o)
                    centre = jnp.where(chosen, q[at + o], centre)
                    left = jnp.where(chosen, edge[at + o], left)
                    right = jnp.where(chosen, edge[at + o + 1], right)
                curve = 6.0 * centre - 3.0 * (left + right)
                value[pl.ds(k * band + s, SUB), :] = left + wk * (
                    (right - left) + curve * (1.0 - wk)
                )
        for r in range(rows):
            for c in range(cols):
                out[f, r, :, c * LANES : (c + 1) * LANES] = value[
                    pl.ds(r * cols + c, levels, stride=band), :
                ]

    loop(0, count, remap)
    for d in range(1, chips - 1):

        @pl.when(chip + d < chips)
        def _():
            sum_copy(d).wait_recv()

    @pl.when(chip == 0)
    def _():
        for c in range(2):
            far_arrival(c).wait_recv()

    for s in starts(band):
        below = surf[pl.ds(s, SUB), :]
        for here, more in (
            (core == 0, psum[pl.ds(s, SUB), :]),
            *((chip + d < chips, sums[d, pl.ds(s, SUB), :]) for d in range(1, chips - 1)),
            *((chip == 0, sums[chips - 1 + c, pl.ds(s, SUB), :]) for c in range(2)),
        ):
            below = below + jnp.where(here, more, jnp.zeros_like(more))
        for k in range(levels - 1, -1, -1):
            term = heat(k, s)
            value[pl.ds(k * band + s, SUB), :] = below + 0.5 * term
            below = below + term
    for r in range(rows):
        for c in range(cols):
            geo[r, :, c * LANES : (c + 1) * LANES] = value[
                pl.ds(r * cols + c, levels, stride=band), :
            ]

    pair_copy().wait_send()

    @pl.when(chip == chips - 1)
    def _():
        for c in range(2):
            far_copy(c).wait_send()

    for d in range(1, chips - 1):

        @pl.when(chip >= d)
        def _():
            sum_copy(d).wait_send()


def leave(out, geo, h_out, h_geo, sems):
    copies = [
        pltpu.make_async_copy(a, b, sems.at[n])
        for n, (a, b) in enumerate(((out, h_out), (geo, h_geo)))
    ]
    for c in copies:
        c.start()
    for c in copies:
        c.wait()


def fused(lats, levs, *args):
    state, courant, offsets, thickness, surface, level, weight = args
    count, rows, levels, width = state.shape
    piece = level.shape[2]
    cols = width // LANES
    band = rows * cols
    slab = band * lats
    room = -(-(slab + 2 * (-(-2 * cols // SUB) * SUB)) // SUB) * SUB
    f32 = jnp.float32
    dma = pltpu.SemaphoreType.DMA

    def tall(n):
        return pltpu.VMEM((-(-n // SUB) * SUB, LANES), f32)

    results = pl.pallas_call(
        functools.partial(kernel, lats, levs),
        out_shape=(pltpu.VMEM(state.shape, f32), pltpu.VMEM(thickness.shape, f32)),
        in_specs=[pl.BlockSpec(memory_space=pl.ANY)] * 7,
        scratch_shapes=[
            *(pltpu.VMEM(x.shape, x.dtype) for x in args),
            tall(levels * count * band),
            tall(levels * 4 * band),
            tall(4 * room),
            tall(count * room),
            tall(room),
            tall(9 * slab),
            tall(count * slab),
            tall(count * (levels + 2 * MARGIN) * band),
            pltpu.VMEM((levs, 2, rows, levels, piece), f32),
            pltpu.VMEM((levs, 2, rows, levels, piece), f32),
            pltpu.VMEM((2, rows, levels, width), f32),
            tall(levels * band),
            tall(levels * band),
            tall(levels * band),
            tall(band),
            tall(band),
            tall(band),
            tall(band),
            pltpu.VMEM((levs // 2 + 1, -(-band // SUB) * SUB, LANES), f32),
            tall(levels * band),
            dma((7,)),
            dma((count + 4, lats)),
            dma((count + 4, lats)),
            dma((count, lats)),
            dma((count, lats)),
            dma((count, 2, lats)),
            dma((count, 2, lats)),
            dma((levs, 2)),
            dma((levs, 2)),
            dma,
            dma,
            dma((levs // 2 + 1,)),
            dma((levs // 2 + 1,)),
            pltpu.SemaphoreType.REGULAR((2, levs // 2)),
            pltpu.SemaphoreType.REGULAR((lats,)),
        ],
        compiler_params=pltpu.CompilerParams(collective_id=0, has_side_effects=True),
    )(*args)
    results = [pltpu.with_memory_space_constraint(x, pltpu.VMEM) for x in results]
    return pl.pallas_call(
        leave,
        out_shape=tuple(pltpu.HBM(x.shape, x.dtype) for x in results),
        in_specs=[pl.BlockSpec(memory_space=pltpu.VMEM)] * 2,
        out_specs=(pl.BlockSpec(memory_space=pltpu.HBM),) * 2,
        scratch_shapes=[dma((2,))],
    )(*results)


def solution(mesh):
    in_specs = (
        P(None, "lat", "lev", None),
        P(None, "lat", "lev", None),
        P(None, "lat", "lev", None),
        P("lat", "lev", None),
        P("lat", None),
        P("lat", None, "lev"),
        P("lat", None, "lev"),
    )
    out_specs = (P(None, "lat", "lev", None), P("lat", "lev", None))
    lats, levs = mesh.shape["lat"], mesh.shape["lev"]

    def body(state, *rest):
        count, rows, levels, width = state.shape
        small = width % LANES or rows * (width // LANES) < SUB
        if levels != lats or levels != MARGIN or small or levs % 2 or levs < 4 or count < 2:
            return per_device(state, *rest)
        return fused(lats, levs, state, *rest)

    return jax.shard_map(
        body, mesh=mesh, in_specs=in_specs, out_specs=out_specs, check_vma=False
    )
```

```python
import functools

import jax
import jax.numpy as jnp
from jax import lax
from jax.experimental import pallas as pl
from jax.experimental.pallas import tpu as pltpu
from jax.sharding import PartitionSpec as P

SUBSTEPS = 2


def extended_2(block, sides, width):
    for axis, dim in sides:
        count = lax.axis_size(axis)
        forward = [(i, i + 1) for i in range(count - 1)]
        backward = [(target, source) for source, target in forward]
        low = lax.ppermute(
            lax.slice_in_dim(block, block.shape[dim] - width, None, axis=dim), axis, forward
        )
        high = lax.ppermute(lax.slice_in_dim(block, 0, width, axis=dim), axis, backward)
        block = jnp.concatenate([low, block, high], axis=dim)
    return block


def from_behind(x, axis, by):
    count = lax.axis_size(axis)
    pairs = [(i, i + by) for i in range(count) if 0 <= i + by < count]
    return lax.ppermute(x, axis, pairs)


def entering(x, axis, combine, identity):
    count, position = (lax.axis_size(axis), lax.axis_index(axis))
    everything = lax.all_gather(x, axis)
    start = jnp.broadcast_to(jnp.asarray(identity, x.dtype), x.shape)

    def lap(k, before):
        at = count - 1 - k
        reached = at > position
        new = combine(before, everything[at])
        return jnp.where(reached, new, before)

    return lax.fori_loop(0, count, lap, start)


def local_parabola(extended, delta, weight):
    margin = 4
    count = extended.shape[-2] - 2 * margin
    edges = (
        7.0 * (extended[..., 1:-2, :] + extended[..., 2:-1, :])
        - (extended[..., :-3, :] + extended[..., 3:, :])
    ) / 12.0
    centre = jnp.zeros(extended.shape[:-2] + (count, extended.shape[-1]), jnp.float32)
    left = centre
    right = centre
    for offset in range(-2, 3):
        chosen = delta == offset
        start = margin + offset
        centre = jnp.where(chosen, extended[..., start : start + count, :], centre)
        left = jnp.where(chosen, edges[..., start - 2 : start - 2 + count, :], left)
        right = jnp.where(chosen, edges[..., start - 1 : start - 1 + count, :], right)
    slope = right - left
    curve = 6.0 * centre - 3.0 * (left + right)
    return left + weight * (slope + curve * (1.0 - weight))


def add_terms(earlier, later):
    return earlier + later


def per_device(state, courant, offsets, log_thickness, surface, remap_level, remap_weight):
    count, rows, levels, width = state.shape
    north_masks = [offsets[0] == offset for offset in range(-1, 3)]
    east_masks = [offsets[1] == offset for offset in range(-1, 3)]
    field = state
    for substep in range(SUBSTEPS):
        padded = extended_2(field, (("lat", 1),), 2)
        picked = jnp.zeros_like(field)
        for number, offset in enumerate(range(-1, 3)):
            picked = jnp.where(
                north_masks[number][None], padded[:, offset + 2 : offset + 2 + rows], picked
            )
        north = courant[0][None] * picked
        below = from_behind(north[:, rows - 1 :], "lat", 1)
        south = jnp.concatenate([below, north[:, : rows - 1]], axis=1)
        moved = jnp.zeros_like(field)
        for number, offset in enumerate(range(-1, 3)):
            moved = jnp.where(east_masks[number][None], jnp.roll(field, -offset, axis=3), moved)
        east = courant[1][None] * moved
        west = jnp.roll(east, 1, axis=3)
        field = field - (north - south) - (east - west)
    heating = field[0] * log_thickness
    lower = [jnp.zeros_like(heating[:, 0])]
    for level in range(levels - 1, 0, -1):
        lower.insert(0, lower[0] + heating[:, level])
    lower_local = jnp.stack(lower, axis=1)
    column_sum = jnp.sum(heating, axis=1)
    deeper = entering(column_sum, "lev", add_terms, jnp.zeros_like(column_sum))
    geopotential = surface[:, None, :] + deeper[:, None, :] + lower_local + 0.5 * heating
    total_levels = remap_level.shape[1]
    delta_col = (remap_level - jnp.arange(total_levels, dtype=jnp.int32)[None, :, None]).astype(
        jnp.float32
    )
    inputs = lax.all_to_all(
        jnp.stack([delta_col, remap_weight]), "lev", split_axis=2, concat_axis=3, tiled=True
    )
    margin = 4
    lev = lax.axis_index("lev")
    before = from_behind(field, "lev", 1)[:, :, levels - margin :]
    after = from_behind(field, "lev", -1)[:, :, :margin]
    before = jnp.where(lev == 0, field[:, :, :1], before)
    after = jnp.where(lev == lax.axis_size("lev") - 1, field[:, :, levels - 1 :], after)
    extended = jnp.concatenate([before, field, after], axis=2)
    remapped = local_parabola(extended, inputs[0][None], inputs[1][None])
    return (remapped, geopotential)


MARGIN = 4
FIRST_DOWN, LAST_UP, LAST_DOWN = 1, 0, 4
LANES = 128
SUB = 8
MESH = pl.DeviceIdType.MESH


def remote(src, dst, send, recv, axis, peer, other=None):
    return pltpu.make_async_remote_copy(
        src_ref=src,
        dst_ref=dst,
        send_sem=send,
        recv_sem=recv,
        device_id={axis: peer, **(other or {})},
        device_id_type=MESH,
    )


def starts(count):
    return [min(at, count - SUB) for at in range(0, count, SUB)]


def copy_rows(target, to, source, at, count):
    for s in starts(count):
        target[pl.ds(to + s, SUB), :] = source[pl.ds(at + s, SUB), :]


def kernel(lats, levs, *refs):
    (
        h_state,
        h_courant,
        h_offsets,
        h_thickness,
        h_surface,
        h_level,
        h_weight,
        out,
        geo,
        state,
        courant,
        offsets,
        thickness,
        surface,
        remap_level,
        remap_weight,
        pack,
        pack_c,
        work_c,
        work,
        mid,
        taps,
        ret,
        ext,
        rpack,
        rrecv,
        rall,
        delta,
        weight,
        thick,
        surf,
        hsum,
        psum,
        csum,
        sums,
        value,
        ins,
        fs,
        fr,
        bs,
        br,
        zs,
        zr,
        rs,
        rr,
        ps,
        pr,
        ss,
        sr,
        far,
        side,
    ) = refs
    count, rows, levels, width = state.shape
    cols = width // LANES
    band = rows * cols
    slab = band * lats
    room = work.shape[0] // count
    low = -(-2 * cols // SUB) * SUB
    deep = (levels + 2 * MARGIN) * band
    piece = remap_level.shape[2]
    plan = [
        (f >= count - LAST_UP, f < FIRST_DOWN or f >= count - LAST_DOWN) for f in range(count)
    ]
    cuts = [f for f in range(1, count) if f == 1 or plan[f] != plan[f - 1]]
    spans = list(zip([0, *cuts], [*cuts, count]))
    me = lax.axis_index("lat")
    lev = lax.axis_index("lev")
    core = lax.rem(lev, 2)
    if lats == 4:
        across = lax.rem(me + 2, lats)
        peers = [lats - 1 - me, across, lats - 1 - across]
    else:
        peers = [lax.rem(me + d, lats) for d in range(1, lats)]

    barrier = pltpu.get_barrier_semaphore()
    chips = levs // 2
    chip = lev // 2
    for peer in peers:
        pl.semaphore_signal(barrier, inc=1, device_id={"lat": peer}, device_id_type=MESH)
    pl.semaphore_signal(
        barrier, inc=1, device_id={"lev": lev + 1 - 2 * core}, device_id_type=MESH
    )

    def near(step):
        return jnp.logical_and(chip + step >= 0, chip + step < chips)

    for step in (-1, 1):
        for c in range(2):

            @pl.when(near(step))
            def _():
                pl.semaphore_signal(
                    barrier,
                    inc=1,
                    device_id={"lev": jnp.clip(2 * (chip + step) + c, 0, levs - 1)},
                    device_id_type=MESH,
                )

    loads = [
        pltpu.make_async_copy(a, b, ins.at[n])
        for n, (a, b) in enumerate(
            (
                (h_courant, courant),
                (h_offsets, offsets),
                (h_state, state),
                (h_level, remap_level),
                (h_weight, remap_weight),
                (h_thickness, thickness),
                (h_surface, surface),
            )
        )
    ]
    for c in loads:
        c.start()

    def spread(target, first, stride, tile, where):
        for c in range(cols):
            target[pl.ds(first + c, tile.shape[-2], stride=stride), :] = tile[
                (*where, slice(None), slice(c * LANES, (c + 1) * LANES))
            ]

    for c in loads[:3]:
        c.wait()
    for r in range(rows):
        for g in range(2):
            for c in range(cols):
                lanes = slice(c * LANES, (c + 1) * LANES)
                pack_c[pl.ds(g * band + r * cols + c, levels, stride=4 * band), :] = courant[
                    g, r, :, lanes
                ]
                pack_c[pl.ds((g + 2) * band + r * cols + c, levels, stride=4 * band), :] = offsets[
                    g, r, :, lanes
                ].astype(jnp.float32)
    for f in range(count):
        for r in range(rows):
            spread(pack, f * band + r * cols, count * band, state, (f, r))

    sides = (chip > 0).astype(jnp.int32) + (chip < chips - 1).astype(jnp.int32)
    pl.semaphore_wait(barrier, len(peers) + 1 + 2 * sides)

    def coefficient_copy(n):
        return [
            remote(
                pack_c.at[pl.ds((peers[n] * 4 + g) * band, band)],
                work_c.at[pl.ds(g * room + low + band * me, band)],
                fs.at[count + g, n],
                fr.at[count + g, n],
                "lat",
                peers[n],
            )
            for g in range(4)
        ]

    def field_copy(f, n):
        return remote(
            pack.at[pl.ds((peers[n] * count + f) * band, band)],
            work.at[pl.ds(f * room + low + band * me, band)],
            fs.at[f, n],
            fr.at[f, n],
            "lat",
            peers[n],
        )

    def back_copy(f, n):
        return remote(
            ret.at[pl.ds(f * slab + band * peers[n], band)],
            ext.at[pl.ds(f * deep + (MARGIN + me) * band, band)],
            bs.at[f, n],
            br.at[f, n],
            "lat",
            peers[n],
        )

    def level_copy(f, way, n):
        level = peers[n] if n < len(peers) else me
        target = ((0, MARGIN + levels)[way] + level) * band
        peer = (jnp.minimum(lev + 1, levs - 1), jnp.maximum(lev - 1, 0))[way]
        if n < len(peers):
            source = ext.at[pl.ds(f * deep + (MARGIN + level) * band, band)]
        else:
            source = ret.at[pl.ds(f * slab + level * band, band)]
        return remote(
            source,
            ext.at[pl.ds(f * deep + target, band)],
            zs.at[f, way, n],
            zr.at[f, way, n],
            "lev",
            peer,
        )

    def direct_copy(f, way, n):
        target = ((0, MARGIN + levels)[way] + me) * band
        peer = (jnp.minimum(lev + 1, levs - 1), jnp.maximum(lev - 1, 0))[way]
        return remote(
            ret.at[pl.ds(f * slab + band * peers[n], band)],
            ext.at[pl.ds(f * deep + target, band)],
            zs.at[f, way, n],
            zr.at[f, way, n],
            "lev",
            peer,
            {"lat": peers[n]},
        )

    up = jnp.logical_and(core == 1, lev < levs - 1)
    down = jnp.logical_and(core == 0, lev > 0)

    def direct_start(f, direct):
        for way, here in enumerate((up, down)):
            if direct[way]:

                @pl.when(here)
                def _():
                    for n in ways:
                        direct_copy(f, way, n).start()

    def level_start(f, n, direct):
        @pl.when(core == 0 if direct[0] else lev < levs - 1)
        def _():
            level_copy(f, 0, n).start()

        @pl.when(core == 1 if direct[1] else lev > 0)
        def _():
            level_copy(f, 1, n).start()

    def spread_remap(step):
        for c in range(2):
            if step or c:

                @pl.when(near(step))
                def _():
                    remap_copy(step, c).start()

    def remap_copy(step, c):
        n = chips - 1 + step
        to = jnp.clip(2 * (chip + step) + (c + core) % 2, 0, levs - 1)
        return remote(rpack.at[to], rrecv.at[lev], rs.at[n, c], rr.at[n, c], "lev", to)

    def remap_arrival(step, c):
        n = chips - 1 + step
        return remote(
            rpack.at[lev], rrecv.at[lev], rs.at[n, c], rr.at[n, c], "lev", lev + 1 - 2 * core
        )

    def relay(way, hop):
        step = (1, -1)[way]

        @pl.when(jnp.logical_and(near(step), near(-step * hop)))
        def _():
            pl.semaphore_signal(
                far.at[way, hop],
                inc=1,
                device_id={"lev": jnp.clip(lev + 2 * step, 0, levs - 1)},
                device_id_type=MESH,
            )

    held = pl.ds(0, band)

    def pair_copy():
        return remote(hsum.at[held], psum.at[held], ps, pr, "lev", lev + 1 - 2 * core)

    def sum_copy(d):
        return remote(csum.at[held], sums.at[d, held], ss.at[d], sr.at[d], "lev", jnp.maximum(lev - 2 * d, core))

    def far_copy(c):
        at, to = chips - 1, jnp.maximum(2 * (chip - chips + 1), 0) + (c + core) % 2
        return remote(hsum.at[held], sums.at[at + core, held], ss.at[at + c], sr.at[at + core], "lev", to)

    def far_arrival(c):
        at = chips - 1 + c
        return remote(hsum.at[held], sums.at[at, held], ss.at[at], sr.at[at], "lev", lev + 1 - 2 * core)

    ways = range(len(peers))
    for way in range(2):
        relay(way, 1)
    for n in ways:
        pl.semaphore_signal(
            side.at[n], inc=1, device_id={"lat": peers[n]}, device_id_type=MESH
        )
    for n in ways:
        for c in coefficient_copy(n):
            c.start()
    for f in range(count + 1):
        if f < count:
            field_copy(f, 0).start()
        for n in ways[1:]:
            if f:
                field_copy(f - 1, n).start()

    for c in loads[3:]:
        c.wait()
    for p in range(levs):
        for r in range(rows):
            lo = p * levels
            ks = lo + lax.broadcasted_iota(jnp.int32, (levels, piece), 0)
            rpack[p, 0, r] = (remap_level[r, lo : lo + levels, :] - ks).astype(jnp.float32)
            rpack[p, 1, r] = remap_weight[r, lo : lo + levels, :]
    for r in range(rows):
        spread(thick, r * cols, band, thickness, (r,))
    spread(surf, 0, cols, surface, ())
    blank = jnp.zeros((SUB, LANES), jnp.float32)
    edges = [min(at, room - SUB) for at in (*range(0, low, SUB), *range(low + slab, room, SUB))]
    for f in range(count):
        copy_rows(work, f * room + low + band * me, pack, (me * count + f) * band, band)
        for at in edges:
            work[pl.ds(f * room + at, SUB), :] = blank
    for at in edges:
        mid[pl.ds(at, SUB), :] = blank
        for g in range(4):
            work_c[pl.ds(g * room + at, SUB), :] = blank
    for g in range(4):
        copy_rows(work_c, g * room + low + band * me, pack_c, (me * 4 + g) * band, band)
    rrecv[lev] = rpack[lev]
    for step in (-1, 0, 1):
        spread_remap(step)
    for hop in range(1, chips - 1):
        for way in range(2):
            back = -(hop + 1) if way == 0 else hop + 1

            @pl.when(near(back))
            def _():
                pl.semaphore_wait(far.at[way, hop], 1)

            if hop + 1 < chips - 1:
                relay(way, hop + 1)
            spread_remap(back)

    row = lax.broadcasted_iota(jnp.int32, (SUB, LANES), 0)
    lane = lax.broadcasted_iota(jnp.int32, (SUB, LANES), 1)
    masks = {1: lane == LANES - 1, 2: lane >= LANES - 2, -1: lane < 1, -2: lane < 2}

    def beside(source, base, p, here, shifts):
        found = []
        for way in (1, -1):
            some = [s for s in shifts if s * way > 0]
            if not some:
                continue
            near_by = source[pl.ds(base + p - way, SUB), :]
            at = (-p if way == 1 else cols - 1 - p) % cols
            if at < SUB:
                wrapped = source[pl.ds(base + p - way + way * cols, SUB), :]
                near_by = jnp.where(row == at, wrapped, near_by)
            for s in some:
                mixed = jnp.where(masks[s], near_by, here)
                found.append(pltpu.roll(mixed, s % LANES, 1))
        return found

    def substep(source, base, target, to):
        for p in starts(slab):
            here = source[pl.ds(base + p, SUB), :]
            terms = [here, *beside(source, base, p, here, (1, 2, -1, -2))]
            terms += [source[pl.ds(base + p + d * cols, SUB), :] for d in (-1, -2, 1, 2)]
            products = [taps[pl.ds(g * slab + p, SUB), :] * q for g, q in enumerate(terms)]
            while len(products) > 1:
                pairs = [x + y for x, y in zip(products[::2], products[1::2])]
                products = pairs + products[2 * len(pairs) :]
            target[pl.ds(to + p, SUB), :] = products[0]

    for n in ways:
        for c in coefficient_copy(n):
            c.wait_recv()
    none = jnp.zeros((SUB, LANES), jnp.float32)
    for p in starts(slab):
        c0, c1, o0, o1 = (work_c[pl.ds(g * room + low + p, SUB), :] for g in range(4))
        under, under_o = (work_c[pl.ds(g * room + low + p - cols, SUB), :] for g in (0, 2))
        back, back_o = (
            beside(work_c, g * room + low, p, here, (1,))[0] for g, here in ((1, c1), (3, o1))
        )
        middle = none + 1.0
        for first, near_c, near_o, far_c, far_o in ((1, c1, o1, back, back_o), (5, c0, o0, under, under_o)):
            own = [jnp.where(near_o == float(o), near_c, none) for o in range(-1, 3)]
            other = [jnp.where(far_o == float(o), far_c, none) for o in range(-1, 3)]
            middle = middle + (other[2] - own[1])
            for g, tap in enumerate((other[1] - own[0], other[0], other[3] - own[2], -own[3])):
                taps[pl.ds((first + g) * slab + p, SUB), :] = tap
        taps[pl.ds(p, SUB), :] = middle

    def advect(f, direct):
        for n in ways:
            field_copy(f, n).wait_recv()
        substep(work, f * room + low, mid, low)
        substep(mid, low, ret, f * slab)
        direct_start(f, direct)
        for n in ways:
            back_copy(f, n).start()
        level_start(f, len(peers), (False, False))
        copy_rows(ext, f * deep + (MARGIN + me) * band, ret, f * slab + band * me, band)

    def loop(first, end, body, *rest):
        def step(f, carry):
            body(f, *rest)
            return carry

        lax.fori_loop(first, end, step, 0)

    for n in ways:
        pl.semaphore_wait(side.at[n], 1)
    for start, end in spans:
        loop(start, end, advect, plan[start])

    for n in ways:
        for c in coefficient_copy(n):
            c.wait_send()
        for f in range(count):
            field_copy(f, n).wait_send()
    for step in range(1 - chips, chips):
        for c in range(2):
            if step or c:

                @pl.when(near(-step))
                def _():
                    remap_arrival(step, c).wait_recv()

                @pl.when(near(step))
                def _():
                    remap_copy(step, c).wait_send()

    for p in range(levs):
        rall[:, :, :, p * piece : (p + 1) * piece] = rrecv[p]
    for g, target in enumerate((delta, weight)):
        for r in range(rows):
            spread(target, r * cols, band, rall, (g, r))

    def heat(k, s):
        at = ext[pl.ds((MARGIN + k) * band + s, SUB), :]
        return at * thick[pl.ds(k * band + s, SUB), :]

    def share(f, direct):
        for n in reversed(ways):
            back_copy(f, n).wait_recv()
            level_start(f, n, direct)

    def sent(f):
        for n in ways:
            back_copy(f, n).wait_send()

    for n in ways:
        back_copy(0, n).wait_recv()
    for s in starts(band):
        hsum[pl.ds(s, SUB), :] = functools.reduce(add_terms, [heat(k, s) for k in range(levels)])

    @pl.when(chip == chips - 1)
    def _():
        for c in range(2):
            far_copy(c).start()

    pair_copy().start()
    pair_copy().wait_recv()
    for s in starts(band):
        csum[pl.ds(s, SUB), :] = hsum[pl.ds(s, SUB), :] + psum[pl.ds(s, SUB), :]
    for d in range(1, chips - 1):

        @pl.when(chip >= d)
        def _():
            sum_copy(d).start()

    for n in ways:
        level_start(0, n, plan[0])
    for start, end in spans[1:]:
        loop(start, end, share, plan[start])
    loop(0, count, sent)

    def remap(f):
        base = f * deep

        @pl.when(lev > 0)
        def _():
            for n in range(lats):
                level_copy(f, 0, n).wait_recv()
                level_copy(f, 1, n).wait_send()

        @pl.when(lev < levs - 1)
        def _():
            for n in range(lats):
                level_copy(f, 1, n).wait_recv()
                level_copy(f, 0, n).wait_send()

        @pl.when(lev == 0)
        def _():
            for m in range(MARGIN):
                copy_rows(ext, base + m * band, ext, base + MARGIN * band, band)

        @pl.when(lev == levs - 1)
        def _():
            end = base + (MARGIN + levels) * band
            for m in range(MARGIN):
                copy_rows(ext, end + m * band, ext, end - band, band)

        for s in starts(band):
            q = [ext[pl.ds(base + m * band + s, SUB), :] for m in range(levels + 2 * MARGIN)]
            edge = {
                m: (7.0 * (q[m - 1] + q[m]) - (q[m - 2] + q[m + 1])) * (1.0 / 12.0)
                for m in range(2, levels + 2 * MARGIN - 1)
            }
            for k in range(levels):
                dk = delta[pl.ds(k * band + s, SUB), :]
                wk = weight[pl.ds(k * band + s, SUB), :]
                at = k + MARGIN
                centre, left, right = q[at - 2], edge[at - 2], edge[at - 1]
                for o in range(-1, 3):
                    chosen = dk == float(o)
                    centre = jnp.where(chosen, q[at + o], centre)
                    left = jnp.where(chosen, edge[at + o], left)
                    right = jnp.where(chosen, edge[at + o + 1], right)
                curve = 6.0 * centre - 3.0 * (left + right)
                value[pl.ds(k * band + s, SUB), :] = left + wk * (
                    (right - left) + curve * (1.0 - wk)
                )
        for r in range(rows):
            for c in range(cols):
                out[f, r, :, c * LANES : (c + 1) * LANES] = value[
                    pl.ds(r * cols + c, levels, stride=band), :
                ]

    loop(0, count, remap)
    for d in range(1, chips - 1):

        @pl.when(chip + d < chips)
        def _():
            sum_copy(d).wait_recv()

    @pl.when(chip == 0)
    def _():
        for c in range(2):
            far_arrival(c).wait_recv()

    for s in starts(band):
        below = surf[pl.ds(s, SUB), :]
        for here, more in (
            (core == 0, psum[pl.ds(s, SUB), :]),
            *((chip + d < chips, sums[d, pl.ds(s, SUB), :]) for d in range(1, chips - 1)),
            *((chip == 0, sums[chips - 1 + c, pl.ds(s, SUB), :]) for c in range(2)),
        ):
            below = below + jnp.where(here, more, jnp.zeros_like(more))
        for k in range(levels - 1, -1, -1):
            term = heat(k, s)
            value[pl.ds(k * band + s, SUB), :] = below + 0.5 * term
            below = below + term
    for r in range(rows):
        for c in range(cols):
            geo[r, :, c * LANES : (c + 1) * LANES] = value[
                pl.ds(r * cols + c, levels, stride=band), :
            ]

    pair_copy().wait_send()

    @pl.when(chip == chips - 1)
    def _():
        for c in range(2):
            far_copy(c).wait_send()

    for d in range(1, chips - 1):

        @pl.when(chip >= d)
        def _():
            sum_copy(d).wait_send()


def leave(out, geo, h_out, h_geo, sems):
    copies = [
        pltpu.make_async_copy(a, b, sems.at[n])
        for n, (a, b) in enumerate(((out, h_out), (geo, h_geo)))
    ]
    for c in copies:
        c.start()
    for c in copies:
        c.wait()


def fused(lats, levs, *args):
    state, courant, offsets, thickness, surface, level, weight = args
    count, rows, levels, width = state.shape
    piece = level.shape[2]
    cols = width // LANES
    band = rows * cols
    slab = band * lats
    room = -(-(slab + 2 * (-(-2 * cols // SUB) * SUB)) // SUB) * SUB
    f32 = jnp.float32
    dma = pltpu.SemaphoreType.DMA

    def tall(n):
        return pltpu.VMEM((-(-n // SUB) * SUB, LANES), f32)

    results = pl.pallas_call(
        functools.partial(kernel, lats, levs),
        out_shape=(pltpu.VMEM(state.shape, f32), pltpu.VMEM(thickness.shape, f32)),
        in_specs=[pl.BlockSpec(memory_space=pl.ANY)] * 7,
        scratch_shapes=[
            *(pltpu.VMEM(x.shape, x.dtype) for x in args),
            tall(levels * count * band),
            tall(levels * 4 * band),
            tall(4 * room),
            tall(count * room),
            tall(room),
            tall(9 * slab),
            tall(count * slab),
            tall(count * (levels + 2 * MARGIN) * band),
            pltpu.VMEM((levs, 2, rows, levels, piece), f32),
            pltpu.VMEM((levs, 2, rows, levels, piece), f32),
            pltpu.VMEM((2, rows, levels, width), f32),
            tall(levels * band),
            tall(levels * band),
            tall(levels * band),
            tall(band),
            tall(band),
            tall(band),
            tall(band),
            pltpu.VMEM((levs // 2 + 1, -(-band // SUB) * SUB, LANES), f32),
            tall(levels * band),
            dma((7,)),
            dma((count + 4, lats)),
            dma((count + 4, lats)),
            dma((count, lats)),
            dma((count, lats)),
            dma((count, 2, lats)),
            dma((count, 2, lats)),
            dma((levs, 2)),
            dma((levs, 2)),
            dma,
            dma,
            dma((levs // 2 + 1,)),
            dma((levs // 2 + 1,)),
            pltpu.SemaphoreType.REGULAR((2, levs // 2)),
            pltpu.SemaphoreType.REGULAR((lats,)),
        ],
        compiler_params=pltpu.CompilerParams(collective_id=0, has_side_effects=True),
    )(*args)
    results = [pltpu.with_memory_space_constraint(x, pltpu.VMEM) for x in results]
    return pl.pallas_call(
        leave,
        out_shape=tuple(pltpu.HBM(x.shape, x.dtype) for x in results),
        in_specs=[pl.BlockSpec(memory_space=pltpu.VMEM)] * 2,
        out_specs=(pl.BlockSpec(memory_space=pltpu.HBM),) * 2,
        scratch_shapes=[dma((2,))],
    )(*results)


def solution(mesh):
    in_specs = (
        P(None, "lat", "lev", None),
        P(None, "lat", "lev", None),
        P(None, "lat", "lev", None),
        P("lat", "lev", None),
        P("lat", None),
        P("lat", None, "lev"),
        P("lat", None, "lev"),
    )
    out_specs = (P(None, "lat", "lev", None), P("lat", "lev", None))
    lats, levs = mesh.shape["lat"], mesh.shape["lev"]

    def body(state, *rest):
        count, rows, levels, width = state.shape
        small = width % LANES or rows * (width // LANES) < SUB
        if levels != lats or levels != MARGIN or small or levs % 2 or levs < 4 or count < 2:
            return per_device(state, *rest)
        return fused(lats, levs, state, *rest)

    return jax.shard_map(
        body, mesh=mesh, in_specs=in_specs, out_specs=out_specs, check_vma=False
    )
```
